512 devices in a mesh: row: 64 (over z, y), col: 8 (over x, core).
Axes of the slice: x: 4, y: 8, z: 8, core: 2. Of those that a mesh axis runs over, the one named last changes fastest.
Arguments:
- matrix: float32 [1, 8192, 8, 1024], P(None, 'row', None, 'col'), may hold values from -8 to 8, as said below
Outputs:
- reduced: float32 [1, 8192, 8, 1024], P(None, 'row', None, 'col')
The draws below stay inside these ranges and needn't reach their ends.
Inputs may be any that keep to these rules, and one draw needn't show every extreme that they name: matrix holds a symmetric matrix.
All inputs are finite; a program needn't handle non-finite values.
Results may differ from the reference program's by a relative error of at most 0.0003.
Values sent between devices are 32-bit elements; how exact they have to be, the bound alone decides.
No kernel may reach another device: no remote copies, remote signals or barrier semaphores. Data moves between devices by JAX's collectives and lax.ppermute only.
A program may use at most 64 MiB of HBM per device.

```python
import jax
import jax.numpy as jnp
from jax import lax

TILE = 128
TR_DEV = 1
TC_DEV = 8
ORDER = 8192


def draw_matrix(key, part):
    places = jnp.arange(ORDER, dtype=jnp.int32)
    near = (jnp.abs(places[:, None] - places[None, :]) < 2 * TILE).astype(jnp.float32)
    raw = jax.random.normal(key, (ORDER, ORDER), jnp.float32)
    sym = (raw + raw.T) * 0.70710678
    sym = sym * (1.0 + 3.0 * near)
    sym = jnp.clip(sym, -8.0, 8.0)
    return sym.reshape(TR_DEV, ORDER // TR_DEV, TC_DEV, ORDER // TC_DEV)


def setup_inputs(seed: int = 0) -> dict:
    seeds = jax.random.split(jax.random.key(seed), 2)
    matrix = draw_matrix(jax.random.fold_in(seeds[1], 71), 0)
    return {"matrix": matrix}


def reference(matrix):
    highest = lax.Precision.HIGHEST
    whole = matrix.reshape(ORDER, ORDER)
    panel = whole[TILE:, :TILE]
    gram = jnp.dot(panel.T.astype(jnp.float32), panel.astype(jnp.float32), precision=highest, preferred_element_type=jnp.float32)
    lower = jnp.linalg.cholesky(gram)
    basis = jax.scipy.linalg.solve_triangular(lower, panel.T, lower=True).T
    identity = jnp.eye(TILE, dtype=jnp.float32)
    top = basis[:TILE]
    coupling = jnp.linalg.solve(identity + top.T, identity)
    vectors = jnp.concatenate([jnp.zeros((TILE, TILE), jnp.float32), basis.at[:TILE].add(identity)], axis=0)
    image = jnp.dot(whole.astype(jnp.float32), vectors.astype(jnp.float32), precision=highest, preferred_element_type=jnp.float32)
    middle = jnp.dot(vectors.T.astype(jnp.float32), image.astype(jnp.float32), precision=highest, preferred_element_type=jnp.float32)
    sandwich = jnp.dot(coupling.T, jnp.dot(middle, coupling, precision=highest), precision=highest)
    update = jnp.dot(image, coupling, precision=highest) - 0.5 * jnp.dot(vectors, sandwich, precision=highest)

    def one_block(index):
        start = (index * TILE).astype(jnp.int32)
        rows = lax.dynamic_slice_in_dim(whole, start, TILE, 0)
        upd_rows = lax.dynamic_slice_in_dim(update, start, TILE, 0)
        vec_rows = lax.dynamic_slice_in_dim(vectors, start, TILE, 0)
        first = jnp.dot(upd_rows.astype(jnp.float32), vectors.T.astype(jnp.float32), precision=highest, preferred_element_type=jnp.float32)
        second = jnp.dot(vec_rows.astype(jnp.float32), update.T.astype(jnp.float32), precision=highest, preferred_element_type=jnp.float32)
        return rows - first - second
    blocks = lax.map(one_block, jnp.arange(ORDER // TILE, dtype=jnp.int32))
    return blocks.reshape(matrix.shape)
```

```python
import jax
import jax.numpy as jnp
from jax import lax
from jax.sharding import Mesh, PartitionSpec as P

COL = ("x", "k")
PLANE = ("y", "x", "k")


def product(left, right, contract):
    return lax.dot_general(
        left,
        right,
        (contract, ((), ())),
        precision=lax.Precision.HIGHEST,
        preferred_element_type=jnp.float32,
    )


def spread(block, axis, count):
    whole = jnp.broadcast_to(block[None], (count,) + block.shape)
    return lax.all_to_all(whole, axis, 0, 0, tiled=True)


def per_device(matrix):
    _, width, count, _ = matrix.shape
    side = lax.axis_size("y")
    row = lax.axis_index("z") * side + lax.axis_index("y")
    col = lax.axis_index(COL)
    swap = [(a * side + b, b * side + a) for a in range(side) for b in range(side)]
    piece = width // side
    identity = jnp.eye(width, dtype=jnp.float32)
    local = matrix[0]

    first = spread(local[:, 0, :], COL, side)
    panel_row = first[0] * (row != 0).astype(jnp.float32)
    next_row = first[1]
    panel_own = lax.ppermute(panel_row, PLANE, swap)
    next_own = lax.ppermute(next_row, PLANE, swap)
    panel = spread(panel_own, "z", count)

    part = product(local, panel, ((1, 2), (0, 1)))
    gram_part = product(panel, panel, ((0, 1), (0, 1)))
    both = jnp.concatenate([part, gram_part], axis=0)
    slots = jnp.concatenate(
        [
            jnp.broadcast_to(both[None], (side, 2 * width, width)),
            panel[0].reshape(side, piece, width),
        ],
        axis=1,
    )
    came = lax.all_to_all(slots, COL, 0, 0, tiled=True)
    head_slice = came[1, 2 * width :]
    total = jnp.sum(came[:, : 2 * width], axis=0)
    mixed_row, gram = total[:width], total[width:]
    mixed_own = lax.ppermute(mixed_row, PLANE, swap)

    lower = jnp.linalg.cholesky(gram)
    inverse = jax.scipy.linalg.solve_triangular(lower, identity, lower=True)
    image_own = product(mixed_own, inverse, ((1,), (1,))) + next_own
    image = spread(image_own, "z", count)

    at_col = ((jnp.arange(count) == 0) & (col == 1)).astype(jnp.float32)
    refl_row = product(panel_row, inverse, ((1,), (1,))) + identity * (row == 1)
    image_row = product(mixed_row, inverse, ((1,), (1,))) + next_row
    refl = product(panel, inverse, ((2,), (1,))) + identity[None] * at_col[:, None, None]

    middle_part = product(refl, image, ((0, 1), (0, 1)))
    came = spread(jnp.concatenate([middle_part, head_slice], axis=0), COL, side)
    middle = jnp.sum(came[:, :width], axis=0)
    head = came[:, width:].reshape(width, width)

    shifted = identity + product(inverse, head, ((1,), (1,)))
    normal = product(shifted, shifted, ((0,), (0,)))
    coupling = jax.scipy.linalg.cho_solve(
        (jnp.linalg.cholesky(normal), True), shifted.T
    )
    sandwich = product(coupling, product(middle, coupling, ((1,), (0,))), ((0,), (0,)))
    upd_row = product(image_row, coupling, ((1,), (0,))) - 0.5 * product(
        refl_row, sandwich, ((1,), (0,))
    )
    upd = product(image, coupling, ((2,), (0,))) - 0.5 * product(
        refl, sandwich, ((2,), (0,))
    )
    left = jnp.concatenate([upd_row, refl_row], axis=1)
    right = jnp.concatenate([refl, upd], axis=2)
    result = local - product(left, right, ((1,), (2,)))
    return result[None]


def solution(mesh):
    grid = Mesh(mesh.devices.reshape(8, 8, 4, 2), ("z", "y", "x", "k"))
    spec = P(None, ("z", "y"), None, COL)
    return jax.shard_map(
        per_device, mesh=grid, in_specs=(spec,), out_specs=spec, check_vma=False
    )
```

```python
import jax
import jax.numpy as jnp
from jax import lax
from jax.experimental import pallas as pl
from jax.experimental.pallas import tpu as pltpu
from jax.sharding import Mesh, PartitionSpec as P

COL = ("x", "k")
PLANE = ("y", "x", "k")
BLOCK = 8


def product(left, right, contract):
    return lax.dot_general(
        left,
        right,
        (contract, ((), ())),
        precision=lax.Precision.HIGHEST,
        preferred_element_type=jnp.float32,
    )


def spread(block, axis, count):
    whole = jnp.broadcast_to(block[None], (count,) + block.shape)
    return lax.all_to_all(whole, axis, 0, 0, tiled=True)


def unit(width):
    rows = lax.broadcasted_iota(jnp.int32, (width, width), 0)
    lanes = lax.broadcasted_iota(jnp.int32, (width, width), 1)
    return (rows == lanes).astype(jnp.float32)


def cholesky_kernel(upper_ref, corner_ref, out_ref, work):
    width = out_ref.shape[0]
    half, quarter = width // 2, width // 4
    work[:half, :width] = upper_ref[...]
    work[half : half + quarter, half:width] = corner_ref[:, :half]
    work[half + quarter :, half:width] = corner_ref[:, half:]
    work[half:, :half] = jnp.zeros((half, half), jnp.float32)
    work[:, width:] = unit(width)
    place = lax.broadcasted_iota(jnp.int32, (BLOCK, 1), 0)
    for low in range(0, width, BLOCK):
        rows = work[low : low + BLOCK, :]
        wide = (BLOCK, width)
        cols = [
            jnp.broadcast_to(rows[:, low + b : low + b + 1], wide) for b in range(BLOCK)
        ]
        for j in range(BLOCK):
            scale = lax.rsqrt(jnp.broadcast_to(cols[j][j : j + 1, :], wide))
            factor = jnp.where(place > j, cols[j] * scale, 0.0)
            for b in range(j + 1, BLOCK):
                pivot = jnp.broadcast_to(cols[b][j : j + 1, :], wide) * scale
                cols[b] = cols[b] - factor * pivot
            pivot = jnp.broadcast_to(rows[j : j + 1, :], rows.shape)
            pivot = pivot * jnp.concatenate([scale, scale], axis=1)
            factor = jnp.concatenate([factor, factor], axis=1)
            rows = jnp.where(place == j, pivot, rows - factor * pivot)
        out_ref[low : low + BLOCK, :] = rows[:, width:]
        if low + BLOCK < width:
            below = rows[:, low + BLOCK : width]
            work[low + BLOCK :, :] = work[low + BLOCK :, :] - product(
                below, rows, ((0,), (0,))
            )


def inverse_kernel(matrix_ref, out_ref, work):
    width = out_ref.shape[0]
    work[:, :width] = matrix_ref[...]
    work[:, width:] = unit(width)
    place = lax.broadcasted_iota(jnp.int32, (BLOCK, 1), 0)
    for low in range(0, width, BLOCK):
        rows = work[low : low + BLOCK, :]
        wide = (BLOCK, width)
        cols = [
            jnp.broadcast_to(rows[:, low + b : low + b + 1], wide) for b in range(BLOCK)
        ]
        for j in range(BLOCK):
            scale = 1.0 / jnp.broadcast_to(cols[j][j : j + 1, :], wide)
            factor = jnp.where(place != j, cols[j], 0.0)
            for b in range(j + 1, BLOCK):
                pivot = jnp.broadcast_to(cols[b][j : j + 1, :], wide) * scale
                cols[b] = jnp.where(place == j, pivot, cols[b] - factor * pivot)
            pivot = jnp.broadcast_to(rows[j : j + 1, :], rows.shape)
            pivot = pivot * jnp.concatenate([scale, scale], axis=1)
            factor = jnp.concatenate([factor, factor], axis=1)
            rows = jnp.where(place == j, pivot, rows - factor * pivot)
        own = unit(width)[:, low : low + BLOCK]
        work[...] = work[...] - product(
            work[:, low : low + BLOCK] - own, rows, ((1,), (0,))
        )
    out_ref[...] = work[:, width:]


def factor_call(kernel, *operands):
    width = operands[0].shape[1]
    return pl.pallas_call(
        kernel,
        out_shape=jax.ShapeDtypeStruct((width, width), jnp.float32),
        scratch_shapes=[pltpu.VMEM((width, 2 * width), jnp.float32)],
        cost_estimate=pl.CostEstimate(
            flops=0, bytes_accessed=30_000_000, transcendentals=0
        ),
        compiler_params=pltpu.CompilerParams(vmem_limit_bytes=4 << 20),
    )(*operands)


def per_device(matrix):
    _, width, count, _ = matrix.shape
    side = lax.axis_size("y")
    row = lax.axis_index("z") * side + lax.axis_index("y")
    col = lax.axis_index(COL)
    swap = [(a * side + b, b * side + a) for a in range(side) for b in range(side)]
    piece, half, quarter = width // side, width // 2, width // 4
    identity = jnp.eye(width, dtype=jnp.float32)
    local = matrix[0]

    first = spread(local[:, 0, :], COL, side)
    panel_row = first[0] * (row != 0).astype(jnp.float32)
    next_row = first[1]
    panel_own = lax.ppermute(panel_row, PLANE, swap)
    panel_own, next_row = lax.optimization_barrier((panel_own, next_row))
    next_own = lax.ppermute(next_row, PLANE, swap)
    panel = spread(panel_own, "z", count)

    part = product(local, panel, ((1, 2), (0, 1)))
    gram_part = product(panel, panel, ((0, 1), (0, 1)))
    shared = jnp.concatenate(
        [
            part,
            gram_part[:half],
            jnp.concatenate(
                [
                    gram_part[half : half + quarter, half:],
                    gram_part[half + quarter :, half:],
                ],
                axis=1,
            ),
        ],
        axis=0,
    )
    tall = shared.shape[0]
    slots = jnp.concatenate(
        [
            jnp.broadcast_to(shared[None], (side, tall, width)),
            panel[0].reshape(side, piece, width),
        ],
        axis=1,
    )
    came = lax.all_to_all(slots, COL, 0, 0, tiled=True)
    total = jnp.sum(came[:, :tall], axis=0)
    mixed_row = total[:width]
    mixed_own = lax.ppermute(mixed_row, PLANE, swap)
    head = spread(came[1, tall:], COL, side).reshape(width, width)
    inverse = factor_call(
        cholesky_kernel, total[width : width + half], total[width + half :]
    )

    image_own = product(mixed_own, inverse, ((1,), (1,))) + next_own
    image = spread(image_own, "z", count)

    coupling = factor_call(
        inverse_kernel, identity + product(inverse, head, ((1,), (1,)))
    )
    at_col = ((jnp.arange(count) == 0) & (col == 1)).astype(jnp.float32)
    refl_row = product(panel_row, inverse, ((1,), (1,))) + identity * (row == 1)
    image_row = product(mixed_row, inverse, ((1,), (1,))) + next_row
    refl = product(panel, inverse, ((2,), (1,))) + identity[None] * at_col[:, None, None]
    half_row = product(image_row, coupling, ((1,), (0,)))
    turned_row = product(refl_row, coupling, ((1,), (1,)))
    turned = product(refl, coupling, ((2,), (1,)))

    middle_part = product(refl, image, ((0, 1), (0, 1)))
    came = spread(middle_part, COL, side)
    half_col = product(image, coupling, ((2,), (0,)))
    left = jnp.concatenate([half_row, refl_row], axis=1)
    right = jnp.concatenate([refl, half_col], axis=2)
    partial = lax.optimization_barrier(local - product(left, right, ((1,), (2,))))

    middle = jnp.sum(came, axis=0)
    turned_row = product(turned_row, middle, ((1,), (0,)))
    result = partial + product(turned_row, turned, ((1,), (2,)))
    return result[None]


def solution(mesh):
    grid = Mesh(mesh.devices.reshape(8, 8, 4, 2), ("z", "y", "x", "k"))
    spec = P(None, ("z", "y"), None, COL)

    return jax.shard_map(
        per_device, mesh=grid, in_specs=(spec,), out_specs=spec, check_vma=False
    )
```

```python
import jax
import jax.numpy as jnp
from jax import lax
from jax.experimental import pallas as pl
from jax.experimental.pallas import tpu as pltpu
from jax.sharding import Mesh, PartitionSpec as P

COL = ("x", "k")
PLANE = ("y", "x", "k")
BLOCK = 8


def product(left, right, contract):
    return lax.dot_general(
        left,
        right,
        (contract, ((), ())),
        precision=lax.Precision.HIGHEST,
        preferred_element_type=jnp.float32,
    )


def spread(block, axis, count):
    whole = jnp.broadcast_to(block[None], (count,) + block.shape)
    return lax.all_to_all(whole, axis, 0, 0, tiled=True)


def unit(width):
    rows = lax.broadcasted_iota(jnp.int32, (width, width), 0)
    lanes = lax.broadcasted_iota(jnp.int32, (width, width), 1)
    return (rows == lanes).astype(jnp.float32)


def cholesky_kernel(upper_ref, corner_ref, out_ref, work):
    width = out_ref.shape[0]
    half, quarter = width // 2, width // 4
    work[:half, :width] = upper_ref[...]
    work[half : half + quarter, half:width] = corner_ref[:, :half]
    work[half + quarter :, half:width] = corner_ref[:, half:]
    work[half:, :half] = jnp.zeros((half, half), jnp.float32)
    work[:, width:] = unit(width)
    place = lax.broadcasted_iota(jnp.int32, (BLOCK, 1), 0)
    for low in range(0, width, BLOCK):
        rows = work[low : low + BLOCK, :]
        wide = (BLOCK, width)
        cols = [
            jnp.broadcast_to(rows[:, low + b : low + b + 1], wide) for b in range(BLOCK)
        ]
        for j in range(BLOCK):
            scale = lax.rsqrt(jnp.broadcast_to(cols[j][j : j + 1, :], wide))
            factor = jnp.where(place > j, cols[j] * scale, 0.0)
            for b in range(j + 1, BLOCK):
                pivot = jnp.broadcast_to(cols[b][j : j + 1, :], wide) * scale
                cols[b] = cols[b] - factor * pivot
            pivot = jnp.broadcast_to(rows[j : j + 1, :], rows.shape)
            pivot = pivot * jnp.concatenate([scale, scale], axis=1)
            factor = jnp.concatenate([factor, factor], axis=1)
            rows = jnp.where(place == j, pivot, rows - factor * pivot)
        out_ref[low : low + BLOCK, :] = rows[:, width:]
        if low + BLOCK < width:
            below = rows[:, low + BLOCK : width]
            work[low + BLOCK :, :] = work[low + BLOCK :, :] - product(
                below, rows, ((0,), (0,))
            )


def inverse_kernel(matrix_ref, out_ref, work):
    width = out_ref.shape[0]
    work[:, :width] = matrix_ref[...]
    work[:, width:] = unit(width)
    place = lax.broadcasted_iota(jnp.int32, (BLOCK, 1), 0)
    for low in range(0, width, BLOCK):
        rows = work[low : low + BLOCK, :]
        wide = (BLOCK, width)
        cols = [
            jnp.broadcast_to(rows[:, low + b : low + b + 1], wide) for b in range(BLOCK)
        ]
        for j in range(BLOCK):
            scale = 1.0 / jnp.broadcast_to(cols[j][j : j + 1, :], wide)
            factor = jnp.where(place != j, cols[j], 0.0)
            for b in range(j + 1, BLOCK):
                pivot = jnp.broadcast_to(cols[b][j : j + 1, :], wide) * scale
                cols[b] = jnp.where(place == j, pivot, cols[b] - factor * pivot)
            pivot = jnp.broadcast_to(rows[j : j + 1, :], rows.shape)
            pivot = pivot * jnp.concatenate([scale, scale], axis=1)
            factor = jnp.concatenate([factor, factor], axis=1)
            rows = jnp.where(place == j, pivot, rows - factor * pivot)
        own = unit(width)[:, low : low + BLOCK]
        work[...] = work[...] - product(
            work[:, low : low + BLOCK] - own, rows, ((1,), (0,))
        )
    out_ref[...] = work[:, width:]


def factor_call(kernel, *operands):
    width = operands[0].shape[1]
    return pl.pallas_call(
        kernel,
        out_shape=jax.ShapeDtypeStruct((width, width), jnp.float32),
        scratch_shapes=[pltpu.VMEM((width, 2 * width), jnp.float32)],
        cost_estimate=pl.CostEstimate(
            flops=0, bytes_accessed=30_000_000, transcendentals=0
        ),
        compiler_params=pltpu.CompilerParams(vmem_limit_bytes=4 << 20),
    )(*operands)


def per_device(matrix):
    _, width, count, _ = matrix.shape
    side = lax.axis_size("y")
    depth = lax.axis_index("z")
    row = depth * side + lax.axis_index("y")
    col = lax.axis_index(COL)
    swap = [(a * side + b, b * side + a) for a in range(side) for b in range(side)]
    piece, half, quarter = width // side, width // 2, width // 4
    local = matrix[0]

    on_row = lax.optimization_barrier(unit(width) * (row == 1))
    identity = unit(width)

    first = spread(local[:, 0, :], COL, side)
    panel_row = first[0] * (row != 0).astype(jnp.float32)
    next_row = first[1]
    panel_own = lax.ppermute(panel_row, PLANE, swap)
    panel = spread(panel_own, "z", count)
    next_own = lax.ppermute(next_row, PLANE, swap)

    part = product(local, panel, ((1, 2), (0, 1)))
    gram_part = product(panel, panel, ((0, 1), (0, 1)))
    shared = jnp.concatenate(
        [
            part,
            gram_part[:half],
            jnp.concatenate(
                [
                    gram_part[half : half + quarter, half:],
                    gram_part[half + quarter :, half:],
                ],
                axis=1,
            ),
            lax.dynamic_slice_in_dim(panel[0], depth * piece, piece, 0),
        ],
        axis=0,
    )
    came = spread(shared, COL, side)
    tall = shared.shape[0] - piece
    total = jnp.sum(came[:, :tall], axis=0)
    head_slice = came[1, tall:]
    mixed_row = total[:width]
    mixed_own = lax.ppermute(mixed_row, PLANE, swap)
    inverse = factor_call(
        cholesky_kernel, total[width : width + half], total[width + half :]
    )

    image_own = product(mixed_own, inverse, ((1,), (1,))) + next_own
    came = spread(jnp.concatenate([image_own, head_slice], axis=0), "z", count)
    image = came[:, :width]
    head = came[:, width:].reshape(width, width)

    at_col = ((jnp.arange(count) == 0) & (col == 1)).astype(jnp.float32)
    refl_row = product(panel_row, inverse, ((1,), (1,))) + on_row
    image_row = product(mixed_row, inverse, ((1,), (1,))) + next_row
    refl = product(panel, inverse, ((2,), (1,))) + identity[None] * at_col[:, None, None]

    middle_part = product(refl, image, ((0, 1), (0, 1)))
    came = spread(middle_part, COL, side)

    coupling = factor_call(
        inverse_kernel, identity + product(inverse, head, ((1,), (1,)))
    )
    turned_row = product(refl_row, coupling, ((1,), (1,)))
    half_row = product(image_row, coupling, ((1,), (0,)))
    partial = lax.optimization_barrier(local - product(turned_row, image, ((1,), (2,))))

    middle = jnp.sum(came, axis=0)
    sandwich_row = product(
        product(turned_row, middle, ((1,), (0,))), coupling, ((1,), (0,))
    )
    result = partial - product(half_row - sandwich_row, refl, ((1,), (2,)))
    return result[None]


def solution(mesh):
    grid = Mesh(mesh.devices.reshape(8, 8, 4, 2), ("z", "y", "x", "k"))
    spec = P(None, ("z", "y"), None, COL)

    return jax.shard_map(
        per_device, mesh=grid, in_specs=(spec,), out_specs=spec, check_vma=False
    )
```

```python
import jax
import jax.numpy as jnp
from jax import lax
from jax.experimental import pallas as pl
from jax.experimental.pallas import tpu as pltpu
from jax.sharding import Mesh, PartitionSpec as P

COL = ("x", "k")
PLANE = ("y", "x", "k")
BLOCK = 8
GROUP = 32


def product(left, right, contract):
    return lax.dot_general(
        left,
        right,
        (contract, ((), ())),
        precision=lax.Precision.HIGHEST,
        preferred_element_type=jnp.float32,
    )


def spread(block, axis, count):
    whole = jnp.broadcast_to(block[None], (count,) + block.shape)
    return lax.all_to_all(whole, axis, 0, 0, tiled=True)


def packed(square):
    half = square.shape[0] // 2
    corner = square[half:, half:]
    corner = jnp.concatenate([corner[: half // 2], corner[half // 2 :]], axis=1)
    return jnp.concatenate([square[:half], corner], axis=0)


def unit(width):
    rows = lax.broadcasted_iota(jnp.int32, (width, width), 0)
    lanes = lax.broadcasted_iota(jnp.int32, (width, width), 1)
    return (rows == lanes).astype(jnp.float32)


def columns_of(rows, low, width):
    return [
        jnp.broadcast_to(rows[:, low + b : low + b + 1], (BLOCK, width))
        for b in range(BLOCK)
    ]


def row_of(rows, j):
    return jnp.broadcast_to(rows[j : j + 1, :], rows.shape)


def cholesky_kernel(upper_ref, corner_ref, out_ref):
    width = out_ref.shape[0]
    half = width // 2
    upper, corner = upper_ref[...], corner_ref[...]
    lower = jnp.concatenate(
        [jnp.zeros((half, half), jnp.float32)]
        + [jnp.concatenate([corner[:, :half], corner[:, half:]], axis=0)],
        axis=1,
    )
    gram = jnp.concatenate([upper, lower], axis=0)
    lanes = lax.broadcasted_iota(jnp.int32, (1, width), 1)
    place = lax.broadcasted_iota(jnp.int32, (BLOCK, 1), 0)
    turned = gram.T
    rows = []
    for low in range(0, width, BLOCK):
        own = gram[low : low + BLOCK, :]
        if low >= half:
            own = jnp.where(lanes < half, turned[low : low + BLOCK, :], own)
        rows.append(own)
    count = width // BLOCK
    for i in range(count):
        low = BLOCK * i
        live = range(i, count)
        cols = {v: columns_of(rows[v], low, width) for v in live}
        inside = (lanes >= low) & (lanes < low + BLOCK)
        for v in live:
            fill = (lanes == low + place).astype(jnp.float32) if v == i else 0.0
            rows[v] = jnp.where(inside, fill, rows[v])
        for j in range(BLOCK):
            scale = lax.rsqrt(row_of(cols[i][j], j))
            pivots = [
                row_of(cols[i][b], j) * scale if b > j else None for b in range(BLOCK)
            ]
            pivot = row_of(rows[i], j) * scale
            for v in live:
                factor = cols[v][j] * scale
                if v == i:
                    factor = jnp.where(place > j, factor, 0.0)
                for b in range(j + 1, BLOCK):
                    cols[v][b] = cols[v][b] - factor * pivots[b]
                after = rows[v] - factor * pivot
                rows[v] = jnp.where(place == j, pivot, after) if v == i else after
        out_ref[low : low + BLOCK, :] = jnp.where(lanes < low + BLOCK, rows[i], 0.0)


def inverse_kernel(matrix_ref, out_ref, work):
    width = out_ref.shape[0]
    work[...] = matrix_ref[...]
    lanes = lax.broadcasted_iota(jnp.int32, (1, width), 1)
    place = lax.broadcasted_iota(jnp.int32, (BLOCK, 1), 0)
    count = GROUP // BLOCK
    for top in range(0, width, GROUP):
        rows = [work[top + BLOCK * v : top + BLOCK * (v + 1), :] for v in range(count)]
        for i in range(count):
            low = top + BLOCK * i
            cols = [columns_of(rows[v], low, width) for v in range(count)]
            inside = (lanes >= low) & (lanes < low + BLOCK)
            for v in range(count):
                fill = (lanes == low + place).astype(jnp.float32) if v == i else 0.0
                rows[v] = jnp.where(inside, fill, rows[v])
            for j in range(BLOCK):
                scale = 1.0 / row_of(cols[i][j], j)
                pivots = [
                    row_of(cols[i][b], j) * scale if b > j else None
                    for b in range(BLOCK)
                ]
                pivot = row_of(rows[i], j) * scale
                for v in range(count):
                    factor = cols[v][j]
                    for b in range(j + 1, BLOCK):
                        after = cols[v][b] - factor * pivots[b]
                        if v == i:
                            after = jnp.where(place == j, pivots[b], after)
                        cols[v][b] = after
                    after = rows[v] - factor * pivot
                    rows[v] = jnp.where(place == j, pivot, after) if v == i else after
        group = jnp.concatenate(rows, axis=0)
        inside = (lanes >= top) & (lanes < top + GROUP)
        for start, stop in ((0, top), (top + GROUP, width)):
            if stop > start:
                old = work[start:stop, :]
                work[start:stop, :] = jnp.where(inside, 0.0, old) - product(
                    old[:, top : top + GROUP], group, ((1,), (0,))
                )
        work[top : top + GROUP, :] = group
    out_ref[...] = work[...]


def transposition(side):
    def ring(a, b, size):
        return min((a - b) % size, (b - a) % size)

    pairs = []
    for c in range(side):
        targets = sorted(range(side), key=lambda y: -ring(y, c, side))
        sources = sorted(range(side), key=lambda d: ring(d // 2, c // 2, side // 2))
        pairs += [(c * side + d, y * side + c) for d, y in zip(sources, targets)]
    return pairs


def factor_call(kernel, scratch, *operands):
    width = operands[0].shape[1]
    return pl.pallas_call(
        kernel,
        out_shape=jax.ShapeDtypeStruct((width, width), jnp.float32),
        scratch_shapes=[pltpu.VMEM((width, width), jnp.float32)] * scratch,
        cost_estimate=pl.CostEstimate(
            flops=0, bytes_accessed=30_000_000, transcendentals=0
        ),
        compiler_params=pltpu.CompilerParams(vmem_limit_bytes=4 << 20),
    )(*operands)


def per_device(matrix):
    _, width, count, _ = matrix.shape
    side = lax.axis_size("y")
    depth = lax.axis_index("z")
    row = depth * side + lax.axis_index("y")
    col = lax.axis_index(COL)
    swap = transposition(side)
    piece, half = width // side, width // 2
    local = matrix[0]

    on_row = lax.optimization_barrier(unit(width) * (row == 1))
    identity = unit(width)

    first = spread(local[:, 0, :], COL, side)
    panel_row = first[0] * (row != 0).astype(jnp.float32)
    next_row = first[1]
    panel_own = lax.ppermute(panel_row, PLANE, swap)
    panel = spread(panel_own, "z", count)
    next_own = lax.ppermute(next_row, PLANE, swap)

    part = product(local, panel, ((1, 2), (0, 1)))
    gram_part = product(panel, panel, ((0, 1), (0, 1)))
    shared = jnp.concatenate(
        [
            part,
            packed(gram_part),
            lax.dynamic_slice_in_dim(panel[0], depth * piece, piece, 0),
        ],
        axis=0,
    )
    came = spread(shared, COL, side)
    tall = shared.shape[0] - piece
    total = jnp.sum(came[:, :tall], axis=0)
    head_slice = came[1, tall:]
    mixed_row = total[:width]
    mixed_own = lax.ppermute(mixed_row, PLANE, swap)
    inverse = factor_call(
        cholesky_kernel, 0, total[width : width + half], total[width + half :]
    )

    image_own = product(mixed_own, inverse, ((1,), (1,))) + next_own
    came = spread(jnp.concatenate([image_own, head_slice], axis=0), "z", count)
    image = came[:, :width]
    head = came[:, width:].reshape(width, width)

    at_col = ((jnp.arange(count) == 0) & (col == 1)).astype(jnp.float32)
    refl_row = product(panel_row, inverse, ((1,), (1,))) + on_row
    image_row = product(mixed_row, inverse, ((1,), (1,))) + next_row
    refl = product(panel, inverse, ((2,), (1,))) + identity[None] * at_col[:, None, None]

    middle_part = packed(product(refl, image, ((0, 1), (0, 1))))
    came = spread(middle_part, COL, side)

    coupling = factor_call(
        inverse_kernel, 1, identity + product(inverse, head, ((1,), (1,)))
    )
    turned_row = product(refl_row, coupling, ((1,), (1,)))
    half_row = product(image_row, coupling, ((1,), (0,)))
    partial = lax.optimization_barrier(local - product(turned_row, image, ((1,), (2,))))

    upper = jnp.sum(came[:, :half], axis=0)
    corner = came[:, half:]
    corner = jnp.concatenate([corner[:, :, :half], corner[:, :, half:]], axis=1)
    corner = jnp.sum(corner, axis=0)
    far = turned_row[:, half:]
    sandwich_row = product(turned_row[:, :half], upper, ((1,), (0,)))
    sandwich_row += jnp.concatenate(
        [
            product(far, upper[:, half:], ((1,), (1,))),
            product(far, corner, ((1,), (0,))),
        ],
        axis=1,
    )
    sandwich_row = product(sandwich_row, coupling, ((1,), (0,)))
    result = partial - product(half_row - sandwich_row, refl, ((1,), (2,)))
    return result[None]


def solution(mesh):
    grid = Mesh(mesh.devices.reshape(8, 8, 4, 2), ("z", "y", "x", "k"))
    spec = P(None, ("z", "y"), None, COL)

    return jax.shard_map(
        per_device, mesh=grid, in_specs=(spec,), out_specs=spec, check_vma=False
    )
```

```python
import jax
import jax.numpy as jnp
from jax import lax
from jax.experimental import pallas as pl
from jax.experimental.pallas import tpu as pltpu
from jax.sharding import Mesh, PartitionSpec as P

COL = ("x", "k")
ROW = ("z", "y")
PLANE = ("y", "x", "k")
BLOCK = 8
GROUP = 32


def product(left, right, contract):
    return lax.dot_general(
        left,
        right,
        (contract, ((), ())),
        precision=lax.Precision.HIGHEST,
        preferred_element_type=jnp.float32,
    )


def spread(block, axis, count):
    whole = jnp.broadcast_to(block[None], (count,) + block.shape)
    return lax.all_to_all(whole, axis, 0, 0, tiled=True)


def packed(square):
    half = square.shape[0] // 2
    corner = square[half:, half:]
    corner = jnp.concatenate([corner[: half // 2], corner[half // 2 :]], axis=1)
    return jnp.concatenate([square[:half], corner], axis=0)


def unit(width):
    rows = lax.broadcasted_iota(jnp.int32, (width, width), 0)
    lanes = lax.broadcasted_iota(jnp.int32, (width, width), 1)
    return (rows == lanes).astype(jnp.float32)


def columns_of(rows, low, width):
    return [
        jnp.broadcast_to(rows[:, low + b : low + b + 1], (BLOCK, width))
        for b in range(BLOCK)
    ]


def row_of(rows, j):
    return jnp.broadcast_to(rows[j : j + 1, :], rows.shape)


def cholesky_kernel(upper_ref, corner_ref, out_ref):
    width = out_ref.shape[0]
    half = width // 2
    upper, corner = upper_ref[...], corner_ref[...]
    lower = jnp.concatenate(
        [jnp.zeros((half, half), jnp.float32)]
        + [jnp.concatenate([corner[:, :half], corner[:, half:]], axis=0)],
        axis=1,
    )
    gram = jnp.concatenate([upper, lower], axis=0)
    lanes = lax.broadcasted_iota(jnp.int32, (1, width), 1)
    place = lax.broadcasted_iota(jnp.int32, (BLOCK, 1), 0)
    turned = gram.T
    rows = []
    for low in range(0, width, BLOCK):
        own = gram[low : low + BLOCK, :]
        if low >= half:
            own = jnp.where(lanes < half, turned[low : low + BLOCK, :], own)
        rows.append(own)
    count = width // BLOCK
    for i in range(count):
        low = BLOCK * i
        live = range(i, count)
        cols = {v: columns_of(rows[v], low, width) for v in live}
        inside = (lanes >= low) & (lanes < low + BLOCK)
        for v in live:
            fill = (lanes == low + place).astype(jnp.float32) if v == i else 0.0
            rows[v] = jnp.where(inside, fill, rows[v])
        for j in range(BLOCK):
            scale = lax.rsqrt(row_of(cols[i][j], j))
            pivots = [
                row_of(cols[i][b], j) * scale if b > j else None for b in range(BLOCK)
            ]
            pivot = row_of(rows[i], j) * scale
            for v in live:
                factor = cols[v][j] * scale
                if v == i:
                    factor = jnp.where(place > j, factor, 0.0)
                for b in range(j + 1, BLOCK):
                    cols[v][b] = cols[v][b] - factor * pivots[b]
                after = rows[v] - factor * pivot
                rows[v] = jnp.where(place == j, pivot, after) if v == i else after
        out_ref[low : low + BLOCK, :] = jnp.where(lanes < low + BLOCK, rows[i], 0.0)


def inverse_kernel(matrix_ref, out_ref, work):
    width = out_ref.shape[0]
    work[...] = matrix_ref[...]
    lanes = lax.broadcasted_iota(jnp.int32, (1, width), 1)
    place = lax.broadcasted_iota(jnp.int32, (BLOCK, 1), 0)
    count = GROUP // BLOCK
    for top in range(0, width, GROUP):
        rows = [work[top + BLOCK * v : top + BLOCK * (v + 1), :] for v in range(count)]
        for i in range(count):
            low = top + BLOCK * i
            cols = [columns_of(rows[v], low, width) for v in range(count)]
            inside = (lanes >= low) & (lanes < low + BLOCK)
            for v in range(count):
                fill = (lanes == low + place).astype(jnp.float32) if v == i else 0.0
                rows[v] = jnp.where(inside, fill, rows[v])
            for j in range(BLOCK):
                scale = 1.0 / row_of(cols[i][j], j)
                pivots = [
                    row_of(cols[i][b], j) * scale if b > j else None
                    for b in range(BLOCK)
                ]
                pivot = row_of(rows[i], j) * scale
                for v in range(count):
                    factor = cols[v][j]
                    for b in range(j + 1, BLOCK):
                        after = cols[v][b] - factor * pivots[b]
                        if v == i:
                            after = jnp.where(place == j, pivots[b], after)
                        cols[v][b] = after
                    after = rows[v] - factor * pivot
                    rows[v] = jnp.where(place == j, pivot, after) if v == i else after
        group = jnp.concatenate(rows, axis=0)
        inside = (lanes >= top) & (lanes < top + GROUP)
        for start, stop in ((0, top), (top + GROUP, width)):
            if stop > start:
                old = work[start:stop, :]
                work[start:stop, :] = jnp.where(inside, 0.0, old) - product(
                    old[:, top : top + GROUP], group, ((1,), (0,))
                )
        work[top : top + GROUP, :] = group
    out_ref[...] = work[...]


def factor_call(kernel, scratch, *operands):
    width = operands[0].shape[1]
    return pl.pallas_call(
        kernel,
        out_shape=jax.ShapeDtypeStruct((width, width), jnp.float32),
        scratch_shapes=[pltpu.VMEM((width, width), jnp.float32)] * scratch,
        cost_estimate=pl.CostEstimate(
            flops=0, bytes_accessed=30_000_000, transcendentals=0
        ),
        compiler_params=pltpu.CompilerParams(vmem_limit_bytes=4 << 20),
    )(*operands)


def per_device(matrix):
    _, width, count, _ = matrix.shape
    side = lax.axis_size("y")
    depth = lax.axis_index("z")
    row = depth * side + lax.axis_index("y")
    col = lax.axis_index(COL)
    swap = [(a * side + b, b * side + a) for a in range(side) for b in range(side)]
    piece, half = width // side, width // 2
    identity = unit(width)
    local = matrix[0]

    start = local[:, 0, :].reshape(side, piece, width)
    turned = lax.all_to_all(start, "y", 0, 0, tiled=True)
    slots = jnp.concatenate([turned, start], axis=1)
    came = lax.all_to_all(slots, COL, 0, 0, tiled=True)
    panel_piece = came[0, :piece] * (depth * side + col != 0)
    next_piece = came[1, :piece]
    panel_slice = came[0, piece:] * (row != 0)
    next_slice = came[1, piece:]
    panel = spread(panel_piece, ROW, side * count).reshape(count, width, width)

    part = product(local, panel, ((1, 2), (0, 1)))
    gram_part = product(panel, panel, ((0, 1), (0, 1)))
    shared = jnp.concatenate([packed(gram_part), panel[0]], axis=0)
    slots = jnp.concatenate(
        [
            part.reshape(side, piece, width),
            jnp.broadcast_to(shared[None], (side,) + shared.shape),
        ],
        axis=1,
    )
    came = lax.all_to_all(slots, COL, 0, 0, tiled=True)
    tall = piece + half + half // 2
    head = came[1, tall:]
    mixed_slice = jnp.sum(came[:, :piece], axis=0)
    total = jnp.sum(came[:, piece:tall], axis=0)
    mixed_piece = lax.ppermute(mixed_slice, PLANE, swap)
    inverse = factor_call(cholesky_kernel, 0, total[:half], total[half:])

    image_piece = product(mixed_piece, inverse, ((1,), (1,))) + next_piece
    image = spread(image_piece, ROW, side * count).reshape(count, width, width)

    coupling = factor_call(
        inverse_kernel, 1, identity + product(inverse, head, ((1,), (1,)))
    )
    at_col = ((jnp.arange(count) == 0) & (col == 1)).astype(jnp.float32)
    refl = product(panel, inverse, ((2,), (1,))) + identity[None] * at_col[:, None, None]
    rows = lax.broadcasted_iota(jnp.int32, (piece, width), 0) + col * piece
    lanes = lax.broadcasted_iota(jnp.int32, (piece, width), 1)
    on_row = ((rows == lanes) & (row == 1)).astype(jnp.float32)
    refl_slice = product(panel_slice, inverse, ((1,), (1,))) + on_row
    image_slice = product(mixed_slice, inverse, ((1,), (1,))) + next_slice
    turned_slice = product(refl_slice, coupling, ((1,), (1,)))
    half_slice = product(image_slice, coupling, ((1,), (0,)))

    middle_part = packed(product(refl, image, ((0, 1), (0, 1))))
    came = spread(
        jnp.concatenate([middle_part, turned_slice, half_slice], axis=0), COL, side
    )
    tall = half + half // 2
    turned_row = came[:, tall : tall + piece].reshape(width, width)
    half_row = came[:, tall + piece :].reshape(width, width)
    upper = jnp.sum(came[:, :half], axis=0)
    corner = came[:, half:tall]
    corner = jnp.concatenate([corner[:, :, :half], corner[:, :, half:]], axis=1)
    corner = jnp.sum(corner, axis=0)
    far = turned_row[:, half:]
    sandwich_row = product(turned_row[:, :half], upper, ((1,), (0,)))
    sandwich_row += jnp.concatenate(
        [
            product(far, upper[:, half:], ((1,), (1,))),
            product(far, corner, ((1,), (0,))),
        ],
        axis=1,
    )
    sandwich_row = product(sandwich_row, coupling, ((1,), (0,)))
    left = jnp.concatenate([half_row - sandwich_row, turned_row], axis=1)
    right = jnp.concatenate([refl, image], axis=2)
    result = local - product(left, right, ((1,), (2,)))
    return result[None]


def solution(mesh):
    grid = Mesh(mesh.devices.reshape(8, 8, 4, 2), ("z", "y", "x", "k"))
    spec = P(None, ("z", "y"), None, COL)

    return jax.shard_map(
        per_device, mesh=grid, in_specs=(spec,), out_specs=spec, check_vma=False
    )
```

```python
import jax
import jax.numpy as jnp
from jax import lax
from jax.experimental import pallas as pl
from jax.experimental.pallas import tpu as pltpu
from jax.sharding import Mesh, PartitionSpec as P

COL = ("x", "k")
PLANE = ("y", "x", "k")
FAST = lax.Precision.HIGH
BLOCK = 8
GROUP = 32


def product(left, right, contract, precision=lax.Precision.HIGHEST):
    return lax.dot_general(
        left,
        right,
        (contract, ((), ())),
        precision=precision,
        preferred_element_type=jnp.float32,
    )


def spread(block, axis, count):
    whole = jnp.broadcast_to(block[None], (count,) + block.shape)
    return lax.all_to_all(whole, axis, 0, 0, tiled=True)


def packed(square):
    half = square.shape[0] // 2
    corner = square[half:, half:]
    corner = jnp.concatenate([corner[: half // 2], corner[half // 2 :]], axis=1)
    return jnp.concatenate([square[:half], corner], axis=0)


def unit(width):
    rows = lax.broadcasted_iota(jnp.int32, (width, width), 0)
    lanes = lax.broadcasted_iota(jnp.int32, (width, width), 1)
    return (rows == lanes).astype(jnp.float32)


def first_kernel(matrix_ref, out_ref, tile, sems):
    tile[...] = matrix_ref[0, :, 0, :]
    copies = [
        pltpu.make_async_copy(tile, out_ref.at[i], sems.at[i])
        for i in range(out_ref.shape[0])
    ]
    for copy in copies:
        copy.start()
    for copy in copies:
        copy.wait()


def first_call(matrix, count):
    width = matrix.shape[-1]
    return pl.pallas_call(
        first_kernel,
        out_shape=jax.ShapeDtypeStruct((count, width, width), jnp.float32),
        in_specs=[pl.BlockSpec(memory_space=pltpu.VMEM)],
        out_specs=pl.BlockSpec(memory_space=pl.ANY),
        scratch_shapes=[
            pltpu.VMEM((width, width), jnp.float32),
            pltpu.SemaphoreType.DMA((count,)),
        ],
        compiler_params=pltpu.CompilerParams(vmem_limit_bytes=2 << 20),
        name="first_tile",
    )(matrix)


def shared_kernel(part_ref, gram_ref, head_ref, out_ref):
    width = part_ref.shape[1]
    half, quarter = width // 2, width // 4
    gram = gram_ref[...]
    out_ref[:width, :] = part_ref[...]
    out_ref[width : width + half, :] = gram[:half]
    corner = [gram[half : half + quarter, half:], gram[half + quarter :, half:]]
    low = width + half
    out_ref[low : low + quarter, :] = jnp.concatenate(corner, axis=1)
    out_ref[low + quarter :, :] = head_ref[...]


def shared_call(part, gram, head):
    width = part.shape[1]
    tall = width + width // 2 + width // 4 + head.shape[0]
    return pl.pallas_call(
        shared_kernel,
        out_shape=jax.ShapeDtypeStruct((tall, width), jnp.float32),
        compiler_params=pltpu.CompilerParams(vmem_limit_bytes=2 << 20),
        name="shared",
    )(part, gram, head)


def columns_of(rows, low, width):
    return [
        jnp.broadcast_to(rows[:, low + b : low + b + 1], (BLOCK, width))
        for b in range(BLOCK)
    ]


def row_of(rows, j):
    return jnp.broadcast_to(rows[j : j + 1, :], rows.shape)


def cholesky_kernel(upper_ref, corner_ref, out_ref):
    width = out_ref.shape[0]
    half = width // 2
    upper, corner = upper_ref[...], corner_ref[...]
    lower = jnp.concatenate(
        [jnp.zeros((half, half), jnp.float32)]
        + [jnp.concatenate([corner[:, :half], corner[:, half:]], axis=0)],
        axis=1,
    )
    gram = jnp.concatenate([upper, lower], axis=0)
    lanes = lax.broadcasted_iota(jnp.int32, (1, width), 1)
    place = lax.broadcasted_iota(jnp.int32, (BLOCK, 1), 0)
    turned = gram.T
    rows = []
    for low in range(0, width, BLOCK):
        own = gram[low : low + BLOCK, :]
        if low >= half:
            own = jnp.where(lanes < half, turned[low : low + BLOCK, :], own)
        rows.append(own)
    count = width // BLOCK
    for i in range(count):
        low = BLOCK * i
        live = range(i, count)
        cols = {v: columns_of(rows[v], low, width) for v in live}
        inside = (lanes >= low) & (lanes < low + BLOCK)
        for v in live:
            fill = (lanes == low + place).astype(jnp.float32) if v == i else 0.0
            rows[v] = jnp.where(inside, fill, rows[v])
        for j in range(BLOCK):
            scale = lax.rsqrt(row_of(cols[i][j], j))
            pivots = [
                row_of(cols[i][b], j) * scale if b > j else None for b in range(BLOCK)
            ]
            pivot = row_of(rows[i], j) * scale
            for v in live:
                factor = cols[v][j] * scale
                if v == i:
                    factor = jnp.where(place > j, factor, 0.0)
                for b in range(j + 1, BLOCK):
                    cols[v][b] = cols[v][b] - factor * pivots[b]
                after = rows[v] - factor * pivot
                rows[v] = jnp.where(place == j, pivot, after) if v == i else after
        out_ref[low : low + BLOCK, :] = jnp.where(lanes < low + BLOCK, rows[i], 0.0)


def inverse_kernel(matrix_ref, out_ref, work):
    width = out_ref.shape[0]
    work[...] = matrix_ref[...]
    lanes = lax.broadcasted_iota(jnp.int32, (1, width), 1)
    place = lax.broadcasted_iota(jnp.int32, (BLOCK, 1), 0)
    count = GROUP // BLOCK
    for top in range(0, width, GROUP):
        rows = [work[top + BLOCK * v : top + BLOCK * (v + 1), :] for v in range(count)]
        for i in range(count):
            low = top + BLOCK * i
            cols = [columns_of(rows[v], low, width) for v in range(count)]
            inside = (lanes >= low) & (lanes < low + BLOCK)
            for v in range(count):
                fill = (lanes == low + place).astype(jnp.float32) if v == i else 0.0
                rows[v] = jnp.where(inside, fill, rows[v])
            for j in range(BLOCK):
                scale = 1.0 / row_of(cols[i][j], j)
                pivots = [
                    row_of(cols[i][b], j) * scale if b > j else None
                    for b in range(BLOCK)
                ]
                pivot = row_of(rows[i], j) * scale
                for v in range(count):
                    factor = cols[v][j]
                    for b in range(j + 1, BLOCK):
                        after = cols[v][b] - factor * pivots[b]
                        if v == i:
                            after = jnp.where(place == j, pivots[b], after)
                        cols[v][b] = after
                    after = rows[v] - factor * pivot
                    rows[v] = jnp.where(place == j, pivot, after) if v == i else after
        group = jnp.concatenate(rows, axis=0)
        inside = (lanes >= top) & (lanes < top + GROUP)
        for start, stop in ((0, top), (top + GROUP, width)):
            if stop > start:
                old = work[start:stop, :]
                work[start:stop, :] = jnp.where(inside, 0.0, old) - product(
                    old[:, top : top + GROUP], group, ((1,), (0,))
                )
        work[top : top + GROUP, :] = group
    out_ref[...] = work[...]


def transposition(side):
    def ring(a, b, size):
        return min((a - b) % size, (b - a) % size)

    pairs = []
    for c in range(side):
        targets = sorted(range(side), key=lambda y: -ring(y, c, side))
        sources = sorted(range(side), key=lambda d: ring(d // 2, c // 2, side // 2))
        pairs += [(c * side + d, y * side + c) for d, y in zip(sources, targets)]
    return pairs


def factor_call(kernel, scratch, *operands):
    width = operands[0].shape[1]
    return pl.pallas_call(
        kernel,
        out_shape=jax.ShapeDtypeStruct((width, width), jnp.float32),
        scratch_shapes=[pltpu.VMEM((width, width), jnp.float32)] * scratch,
        cost_estimate=pl.CostEstimate(
            flops=0, bytes_accessed=30_000_000, transcendentals=0
        ),
        compiler_params=pltpu.CompilerParams(vmem_limit_bytes=4 << 20),
    )(*operands)


def per_device(matrix):
    _, width, count, _ = matrix.shape
    side = lax.axis_size("y")
    depth = lax.axis_index("z")
    row = depth * side + lax.axis_index("y")
    col = lax.axis_index(COL)
    swap = transposition(side)
    piece, half = width // side, width // 2
    local = matrix[0]

    on_row = lax.optimization_barrier(unit(width) * (row == 1))
    identity = unit(width)

    first = lax.all_to_all(first_call(matrix, side), COL, 0, 0, tiled=True)
    panel_row = first[0] * (row != 0).astype(jnp.float32)
    next_row = first[1]
    panel_own = lax.ppermute(panel_row, PLANE, swap)
    panel = spread(panel_own, "z", count)
    next_own = lax.ppermute(next_row, PLANE, swap)

    part = product(local, panel, ((1, 2), (0, 1)))
    gram_part = product(panel, panel, ((0, 1), (0, 1)))
    head_slice = lax.dynamic_slice_in_dim(panel[0], depth * piece, piece, 0)
    shared = shared_call(part, gram_part, head_slice)
    came = spread(shared, COL, side)
    tall = shared.shape[0] - piece
    total = jnp.sum(came[:, :tall], axis=0)
    head_slice = came[1, tall:]
    mixed_row = total[:width]
    mixed_own = lax.ppermute(mixed_row, PLANE, swap)
    inverse = factor_call(
        cholesky_kernel, 0, total[width : width + half], total[width + half :]
    )

    image_own = product(mixed_own, inverse, ((1,), (1,))) + next_own
    came = spread(jnp.concatenate([image_own, head_slice], axis=0), "z", count)
    image = came[:, :width]
    head = came[:, width:].reshape(width, width)

    at_col = ((jnp.arange(count) == 0) & (col == 1)).astype(jnp.float32)
    refl_row = product(panel_row, inverse, ((1,), (1,))) + on_row
    image_row = product(mixed_row, inverse, ((1,), (1,))) + next_row
    refl = product(panel, inverse, ((2,), (1,))) + identity[None] * at_col[:, None, None]

    middle_part = packed(product(refl, image, ((0, 1), (0, 1)), FAST))
    came = spread(middle_part, COL, side)

    coupling = factor_call(
        inverse_kernel, 1, identity + product(inverse, head, ((1,), (1,)))
    )
    turned_row = product(refl_row, coupling, ((1,), (1,)))
    half_row = product(image_row, coupling, ((1,), (0,)))
    partial = lax.optimization_barrier(local - product(turned_row, image, ((1,), (2,)), FAST))

    upper = jnp.sum(came[:, :half], axis=0)
    corner = came[:, half:]
    corner = jnp.concatenate([corner[:, :, :half], corner[:, :, half:]], axis=1)
    corner = jnp.sum(corner, axis=0)
    far = turned_row[:, half:]
    sandwich_row = product(turned_row[:, :half], upper, ((1,), (0,)))
    sandwich_row += jnp.concatenate(
        [
            product(far, upper[:, half:], ((1,), (1,))),
            product(far, corner, ((1,), (0,))),
        ],
        axis=1,
    )
    sandwich_row = product(sandwich_row, coupling, ((1,), (0,)))
    result = partial - product(half_row - sandwich_row, refl, ((1,), (2,)), FAST)
    return result[None]


def solution(mesh):
    grid = Mesh(mesh.devices.reshape(8, 8, 4, 2), ("z", "y", "x", "k"))
    spec = P(None, ("z", "y"), None, COL)

    return jax.shard_map(
        per_device, mesh=grid, in_specs=(spec,), out_specs=spec, check_vma=False
    )
```

```python
import jax
import jax.numpy as jnp
from jax import lax
from jax.experimental import pallas as pl
from jax.experimental.pallas import tpu as pltpu
from jax.sharding import Mesh, PartitionSpec as P

COL = ("x", "k")
PLANE = ("y", "x", "k")
FAST = lax.Precision.HIGH
BLOCK = 8
GROUP = 32


def product(left, right, contract, precision=lax.Precision.HIGHEST):
    return lax.dot_general(
        left,
        right,
        (contract, ((), ())),
        precision=precision,
        preferred_element_type=jnp.float32,
    )


def spread(block, axis, count):
    whole = jnp.broadcast_to(block[None], (count,) + block.shape)
    return lax.all_to_all(whole, axis, 0, 0, tiled=True)


def packed(square):
    half = square.shape[0] // 2
    corner = square[half:, half:]
    corner = jnp.concatenate([corner[: half // 2], corner[half // 2 :]], axis=1)
    return jnp.concatenate([square[:half], corner], axis=0)


def unit(width):
    rows = lax.broadcasted_iota(jnp.int32, (width, width), 0)
    lanes = lax.broadcasted_iota(jnp.int32, (width, width), 1)
    return (rows == lanes).astype(jnp.float32)


def first_kernel(matrix_ref, out_ref, tile, sem, sems):
    take = pltpu.make_async_copy(matrix_ref.at[0, :, 0, :], tile, sem)
    take.start()
    take.wait()
    copies = [
        pltpu.make_async_copy(tile, out_ref.at[i], sems.at[i])
        for i in range(out_ref.shape[0])
    ]
    for copy in copies:
        copy.start()
    for copy in copies:
        copy.wait()


def first_call(matrix, count):
    width = matrix.shape[-1]
    return pl.pallas_call(
        first_kernel,
        out_shape=jax.ShapeDtypeStruct((count, width, width), jnp.float32),
        in_specs=[pl.BlockSpec(memory_space=pltpu.HBM)],
        out_specs=pl.BlockSpec(memory_space=pl.ANY),
        scratch_shapes=[
            pltpu.VMEM((width, width), jnp.float32),
            pltpu.SemaphoreType.DMA,
            pltpu.SemaphoreType.DMA((count,)),
        ],
        compiler_params=pltpu.CompilerParams(vmem_limit_bytes=2 << 20),
        name="first_tile",
    )(pltpu.with_memory_space_constraint(matrix, pltpu.HBM))


def shared_kernel(part_ref, gram_ref, head_ref, out_ref):
    width = part_ref.shape[1]
    half, quarter = width // 2, width // 4
    gram = gram_ref[...]
    out_ref[:width, :] = part_ref[...]
    out_ref[width : width + half, :] = gram[:half]
    corner = [gram[half : half + quarter, half:], gram[half + quarter :, half:]]
    low = width + half
    out_ref[low : low + quarter, :] = jnp.concatenate(corner, axis=1)
    out_ref[low + quarter :, :] = head_ref[...]


def shared_call(part, gram, head):
    width = part.shape[1]
    tall = width + width // 2 + width // 4 + head.shape[0]
    return pl.pallas_call(
        shared_kernel,
        out_shape=jax.ShapeDtypeStruct((tall, width), jnp.float32),
        compiler_params=pltpu.CompilerParams(vmem_limit_bytes=2 << 20),
        name="shared",
    )(part, gram, head)


def columns_of(rows, low, width):
    return [
        jnp.broadcast_to(rows[:, low + b : low + b + 1], (BLOCK, width))
        for b in range(BLOCK)
    ]


def row_of(rows, j):
    return jnp.broadcast_to(rows[j : j + 1, :], rows.shape)


def cholesky_kernel(upper_ref, corner_ref, out_ref):
    width = out_ref.shape[0]
    half = width // 2
    upper, corner = upper_ref[...], corner_ref[...]
    lower = jnp.concatenate(
        [jnp.zeros((half, half), jnp.float32)]
        + [jnp.concatenate([corner[:, :half], corner[:, half:]], axis=0)],
        axis=1,
    )
    gram = jnp.concatenate([upper, lower], axis=0)
    lanes = lax.broadcasted_iota(jnp.int32, (1, width), 1)
    place = lax.broadcasted_iota(jnp.int32, (BLOCK, 1), 0)
    turned = gram.T
    rows = []
    for low in range(0, width, BLOCK):
        own = gram[low : low + BLOCK, :]
        if low >= half:
            own = jnp.where(lanes < half, turned[low : low + BLOCK, :], own)
        rows.append(own)
    count = width // BLOCK
    for i in range(count):
        low = BLOCK * i
        live = range(i, count)
        cols = {v: columns_of(rows[v], low, width) for v in live}
        inside = (lanes >= low) & (lanes < low + BLOCK)
        for v in live:
            fill = (lanes == low + place).astype(jnp.float32) if v == i else 0.0
            rows[v] = jnp.where(inside, fill, rows[v])
        for j in range(BLOCK):
            scale = lax.rsqrt(row_of(cols[i][j], j))
            pivots = [
                row_of(cols[i][b], j) * scale if b > j else None for b in range(BLOCK)
            ]
            pivot = row_of(rows[i], j) * scale
            for v in live:
                factor = cols[v][j] * scale
                if v == i:
                    factor = jnp.where(place > j, factor, 0.0)
                for b in range(j + 1, BLOCK):
                    cols[v][b] = cols[v][b] - factor * pivots[b]
                after = rows[v] - factor * pivot
                rows[v] = jnp.where(place == j, pivot, after) if v == i else after
        out_ref[low : low + BLOCK, :] = jnp.where(lanes < low + BLOCK, rows[i], 0.0)


def inverse_kernel(matrix_ref, out_ref, work):
    width = out_ref.shape[0]
    work[...] = matrix_ref[...]
    lanes = lax.broadcasted_iota(jnp.int32, (1, width), 1)
    place = lax.broadcasted_iota(jnp.int32, (BLOCK, 1), 0)
    count = GROUP // BLOCK
    for top in range(0, width, GROUP):
        rows = [work[top + BLOCK * v : top + BLOCK * (v + 1), :] for v in range(count)]
        for i in range(count):
            low = top + BLOCK * i
            cols = [columns_of(rows[v], low, width) for v in range(count)]
            inside = (lanes >= low) & (lanes < low + BLOCK)
            for v in range(count):
                fill = (lanes == low + place).astype(jnp.float32) if v == i else 0.0
                rows[v] = jnp.where(inside, fill, rows[v])
            for j in range(BLOCK):
                scale = 1.0 / row_of(cols[i][j], j)
                pivots = [
                    row_of(cols[i][b], j) * scale if b > j else None
                    for b in range(BLOCK)
                ]
                pivot = row_of(rows[i], j) * scale
                for v in range(count):
                    factor = cols[v][j]
                    for b in range(j + 1, BLOCK):
                        after = cols[v][b] - factor * pivots[b]
                        if v == i:
                            after = jnp.where(place == j, pivots[b], after)
                        cols[v][b] = after
                    after = rows[v] - factor * pivot
                    rows[v] = jnp.where(place == j, pivot, after) if v == i else after
        group = jnp.concatenate(rows, axis=0)
        inside = (lanes >= top) & (lanes < top + GROUP)
        for start, stop in ((0, top), (top + GROUP, width)):
            if stop > start:
                old = work[start:stop, :]
                work[start:stop, :] = jnp.where(inside, 0.0, old) - product(
                    old[:, top : top + GROUP], group, ((1,), (0,))
                )
        work[top : top + GROUP, :] = group
    out_ref[...] = work[...]


def transposition(side):
    def ring(a, b, size):
        return min((a - b) % size, (b - a) % size)

    pairs = []
    for c in range(side):
        targets = sorted(range(side), key=lambda y: -ring(y, c, side))
        sources = sorted(range(side), key=lambda d: ring(d // 2, c // 2, side // 2))
        pairs += [(c * side + d, y * side + c) for d, y in zip(sources, targets)]
    return pairs


def factor_call(kernel, scratch, *operands):
    width = operands[0].shape[1]
    return pl.pallas_call(
        kernel,
        out_shape=jax.ShapeDtypeStruct((width, width), jnp.float32),
        scratch_shapes=[pltpu.VMEM((width, width), jnp.float32)] * scratch,
        cost_estimate=pl.CostEstimate(
            flops=0, bytes_accessed=30_000_000, transcendentals=0
        ),
        compiler_params=pltpu.CompilerParams(vmem_limit_bytes=4 << 20),
    )(*operands)


def per_device(matrix):
    _, width, count, _ = matrix.shape
    side = lax.axis_size("y")
    depth = lax.axis_index("z")
    row = depth * side + lax.axis_index("y")
    col = lax.axis_index(COL)
    swap = transposition(side)
    piece, half = width // side, width // 2
    local = matrix[0]

    on_row = lax.optimization_barrier(unit(width) * (row == 1))
    identity = unit(width)

    first = lax.all_to_all(first_call(matrix, side), COL, 0, 0, tiled=True)
    panel_row = first[0] * (row != 0).astype(jnp.float32)
    next_row = first[1]
    panel_own = lax.ppermute(panel_row, PLANE, swap)
    near = lax.optimization_barrier(jnp.transpose(local, (1, 0, 2)))
    panel = spread(panel_own, "z", count)
    next_own = lax.ppermute(next_row, PLANE, swap)

    part = product(near, panel, ((0, 2), (0, 1)))
    gram_part = product(panel, panel, ((0, 1), (0, 1)))
    head_slice = lax.dynamic_slice_in_dim(panel[0], depth * piece, piece, 0)
    shared = shared_call(part, gram_part, head_slice)
    came = spread(shared, COL, side)
    tall = shared.shape[0] - piece
    total = jnp.sum(came[:, :tall], axis=0)
    head_slice = came[1, tall:]
    mixed_row = total[:width]
    mixed_own = lax.ppermute(mixed_row, PLANE, swap)
    inverse = factor_call(
        cholesky_kernel, 0, total[width : width + half], total[width + half :]
    )

    image_own = product(mixed_own, inverse, ((1,), (1,))) + next_own
    came = spread(jnp.concatenate([image_own, head_slice], axis=0), "z", count)
    image = came[:, :width]
    head = came[:, width:].reshape(width, width)

    at_col = ((jnp.arange(count) == 0) & (col == 1)).astype(jnp.float32)
    refl_row = product(panel_row, inverse, ((1,), (1,))) + on_row
    image_row = product(mixed_row, inverse, ((1,), (1,))) + next_row
    refl = product(panel, inverse, ((2,), (1,))) + identity[None] * at_col[:, None, None]

    middle_part = packed(product(refl, image, ((0, 1), (0, 1)), FAST))
    came = spread(middle_part, COL, side)

    coupling = factor_call(
        inverse_kernel, 1, identity + product(inverse, head, ((1,), (1,)))
    )
    turned_row = product(refl_row, coupling, ((1,), (1,)))
    half_row = product(image_row, coupling, ((1,), (0,)))
    partial = lax.optimization_barrier(near.transpose(1, 0, 2) - product(turned_row, image, ((1,), (2,)), FAST))

    upper = jnp.sum(came[:, :half], axis=0)
    corner = came[:, half:]
    corner = jnp.concatenate([corner[:, :, :half], corner[:, :, half:]], axis=1)
    corner = jnp.sum(corner, axis=0)
    far = turned_row[:, half:]
    sandwich_row = product(turned_row[:, :half], upper, ((1,), (0,)))
    sandwich_row += jnp.concatenate(
        [
            product(far, upper[:, half:], ((1,), (1,))),
            product(far, corner, ((1,), (0,))),
        ],
        axis=1,
    )
    sandwich_row = product(sandwich_row, coupling, ((1,), (0,)))
    result = partial - product(half_row - sandwich_row, refl, ((1,), (2,)), FAST)
    return result[None]


def solution(mesh):
    grid = Mesh(mesh.devices.reshape(8, 8, 4, 2), ("z", "y", "x", "k"))
    spec = P(None, ("z", "y"), None, COL)

    return jax.shard_map(
        per_device, mesh=grid, in_specs=(spec,), out_specs=spec, check_vma=False
    )
```

```python
import jax
import jax.numpy as jnp
from jax import lax
from jax.experimental import pallas as pl
from jax.experimental.pallas import tpu as pltpu
from jax.sharding import Mesh, PartitionSpec as P

COL = ("x", "k")
PLANE = ("y", "x", "k")
FAST = lax.Precision.HIGH
BLOCK = 8
GROUP = 32


def product(left, right, contract, precision=lax.Precision.HIGHEST):
    return lax.dot_general(
        left,
        right,
        (contract, ((), ())),
        precision=precision,
        preferred_element_type=jnp.float32,
    )


def spread(block, axis, count):
    whole = jnp.broadcast_to(block[None], (count,) + block.shape)
    return lax.all_to_all(whole, axis, 0, 0, tiled=True)


def packed(square):
    half = square.shape[0] // 2
    corner = square[half:, half:]
    corner = jnp.concatenate([corner[: half // 2], corner[half // 2 :]], axis=1)
    return jnp.concatenate([square[:half], corner], axis=0)


def unit(width):
    rows = lax.broadcasted_iota(jnp.int32, (width, width), 0)
    lanes = lax.broadcasted_iota(jnp.int32, (width, width), 1)
    return (rows == lanes).astype(jnp.float32)


def first_kernel(matrix_ref, out_ref, tile, sem, sems):
    take = pltpu.make_async_copy(matrix_ref.at[0, :, 0, :], tile, sem)
    take.start()
    take.wait()
    copies = [
        pltpu.make_async_copy(tile, out_ref.at[i], sems.at[i])
        for i in range(out_ref.shape[0])
    ]
    for copy in copies:
        copy.start()
    for copy in copies:
        copy.wait()


def first_call(matrix, count):
    width = matrix.shape[-1]
    return pl.pallas_call(
        first_kernel,
        out_shape=jax.ShapeDtypeStruct((count, width, width), jnp.float32),
        in_specs=[pl.BlockSpec(memory_space=pltpu.HBM)],
        out_specs=pl.BlockSpec(memory_space=pl.ANY),
        scratch_shapes=[
            pltpu.VMEM((width, width), jnp.float32),
            pltpu.SemaphoreType.DMA,
            pltpu.SemaphoreType.DMA((count,)),
        ],
        compiler_params=pltpu.CompilerParams(vmem_limit_bytes=2 << 20),
        name="first_tile",
    )(pltpu.with_memory_space_constraint(matrix, pltpu.HBM))


def shared_kernel(part_ref, gram_ref, out_ref):
    width = part_ref.shape[1]
    half, quarter = width // 2, width // 4
    gram = gram_ref[...]
    out_ref[:width, :] = part_ref[...]
    out_ref[width : width + half, :] = gram[:half]
    corner = [gram[half : half + quarter, half:], gram[half + quarter :, half:]]
    low = width + half
    out_ref[low:, :] = jnp.concatenate(corner, axis=1)


def shared_call(part, gram):
    width = part.shape[1]
    tall = width + width // 2 + width // 4
    return pl.pallas_call(
        shared_kernel,
        out_shape=jax.ShapeDtypeStruct((tall, width), jnp.float32),
        compiler_params=pltpu.CompilerParams(vmem_limit_bytes=2 << 20),
        name="shared",
    )(part, gram)


def columns_of(rows, low, width):
    return [
        jnp.broadcast_to(rows[:, low + b : low + b + 1], (BLOCK, width))
        for b in range(BLOCK)
    ]


def row_of(rows, j):
    return jnp.broadcast_to(rows[j : j + 1, :], rows.shape)


def cholesky_kernel(upper_ref, corner_ref, out_ref):
    width = out_ref.shape[0]
    half = width // 2
    upper, corner = upper_ref[...], corner_ref[...]
    lower = jnp.concatenate(
        [jnp.zeros((half, half), jnp.float32)]
        + [jnp.concatenate([corner[:, :half], corner[:, half:]], axis=0)],
        axis=1,
    )
    gram = jnp.concatenate([upper, lower], axis=0)
    lanes = lax.broadcasted_iota(jnp.int32, (1, width), 1)
    place = lax.broadcasted_iota(jnp.int32, (BLOCK, 1), 0)
    turned = gram.T
    rows = []
    for low in range(0, width, BLOCK):
        own = gram[low : low + BLOCK, :]
        if low >= half:
            own = jnp.where(lanes < half, turned[low : low + BLOCK, :], own)
        rows.append(own)
    count = width // BLOCK
    for i in range(count):
        low = BLOCK * i
        live = range(i, count)
        cols = {v: columns_of(rows[v], low, width) for v in live}
        inside = (lanes >= low) & (lanes < low + BLOCK)
        for v in live:
            fill = (lanes == low + place).astype(jnp.float32) if v == i else 0.0
            rows[v] = jnp.where(inside, fill, rows[v])
        for j in range(BLOCK):
            scale = lax.rsqrt(row_of(cols[i][j], j))
            pivots = [
                row_of(cols[i][b], j) * scale if b > j else None for b in range(BLOCK)
            ]
            pivot = row_of(rows[i], j) * scale
            for v in live:
                factor = cols[v][j] * scale
                if v == i:
                    factor = jnp.where(place > j, factor, 0.0)
                for b in range(j + 1, BLOCK):
                    cols[v][b] = cols[v][b] - factor * pivots[b]
                after = rows[v] - factor * pivot
                rows[v] = jnp.where(place == j, pivot, after) if v == i else after
        out_ref[low : low + BLOCK, :] = jnp.where(lanes < low + BLOCK, rows[i], 0.0)


def inverse_kernel(matrix_ref, out_ref, work):
    width = out_ref.shape[0]
    work[...] = matrix_ref[...]
    lanes = lax.broadcasted_iota(jnp.int32, (1, width), 1)
    place = lax.broadcasted_iota(jnp.int32, (BLOCK, 1), 0)
    count = GROUP // BLOCK
    for top in range(0, width, GROUP):
        rows = [work[top + BLOCK * v : top + BLOCK * (v + 1), :] for v in range(count)]
        for i in range(count):
            low = top + BLOCK * i
            cols = [columns_of(rows[v], low, width) for v in range(count)]
            inside = (lanes >= low) & (lanes < low + BLOCK)
            for v in range(count):
                fill = (lanes == low + place).astype(jnp.float32) if v == i else 0.0
                rows[v] = jnp.where(inside, fill, rows[v])
            for j in range(BLOCK):
                scale = 1.0 / row_of(cols[i][j], j)
                pivots = [
                    row_of(cols[i][b], j) * scale if b > j else None
                    for b in range(BLOCK)
                ]
                pivot = row_of(rows[i], j) * scale
                for v in range(count):
                    factor = cols[v][j]
                    for b in range(j + 1, BLOCK):
                        after = cols[v][b] - factor * pivots[b]
                        if v == i:
                            after = jnp.where(place == j, pivots[b], after)
                        cols[v][b] = after
                    after = rows[v] - factor * pivot
                    rows[v] = jnp.where(place == j, pivot, after) if v == i else after
        group = jnp.concatenate(rows, axis=0)
        inside = (lanes >= top) & (lanes < top + GROUP)
        for start, stop in ((0, top), (top + GROUP, width)):
            if stop > start:
                old = work[start:stop, :]
                work[start:stop, :] = jnp.where(inside, 0.0, old) - product(
                    old[:, top : top + GROUP], group, ((1,), (0,))
                )
        work[top : top + GROUP, :] = group
    out_ref[...] = work[...]


def transposition(side):
    def ring(a, b, size):
        return min((a - b) % size, (b - a) % size)

    pairs = []
    for c in range(side):
        targets = sorted(range(side), key=lambda y: -ring(y, c, side))
        sources = sorted(range(side), key=lambda d: ring(d // 2, c // 2, side // 2))
        pairs += [(c * side + d, y * side + c) for d, y in zip(sources, targets)]
    return pairs


def factor_call(kernel, scratch, *operands):
    width = operands[0].shape[1]
    return pl.pallas_call(
        kernel,
        out_shape=jax.ShapeDtypeStruct((width, width), jnp.float32),
        scratch_shapes=[pltpu.VMEM((width, width), jnp.float32)] * scratch,
        cost_estimate=pl.CostEstimate(
            flops=0, bytes_accessed=30_000_000, transcendentals=0
        ),
        compiler_params=pltpu.CompilerParams(vmem_limit_bytes=4 << 20),
    )(*operands)


def per_device(matrix):
    _, width, count, _ = matrix.shape
    side = lax.axis_size("y")
    row = lax.axis_index("z") * side + lax.axis_index("y")
    col = lax.axis_index(COL)
    swap = transposition(side)
    half = width // 2
    local = matrix[0]

    on_row = lax.optimization_barrier(unit(width) * (row == 1))
    on_col = lax.optimization_barrier((col == 1).astype(jnp.float32))
    at_col = (jnp.arange(count) == 0).astype(jnp.float32) * on_col
    at_col = lax.optimization_barrier(at_col)
    identity = unit(width)

    first = lax.all_to_all(first_call(matrix, side), COL, 0, 0, tiled=True)
    panel_row = first[0] * (row != 0).astype(jnp.float32)
    next_row = first[1]
    panel_own = lax.ppermute(panel_row, PLANE, swap)
    near = lax.optimization_barrier(jnp.transpose(local, (1, 0, 2)))
    panel = spread(panel_own, "z", count)
    next_own = lax.ppermute(next_row, PLANE, swap)

    part = product(near, panel, ((0, 2), (0, 1)))
    gram_part = product(panel, panel, ((0, 1), (0, 1)))
    shared = shared_call(part, gram_part)
    total = jnp.sum(spread(shared, COL, side), axis=0)
    mixed_row = total[:width]
    mixed_own = lax.ppermute(mixed_row, PLANE, swap)
    inverse = factor_call(
        cholesky_kernel, 0, total[width : width + half], total[width + half :]
    )

    image_own = product(mixed_own, inverse, ((1,), (1,))) + next_own
    image = spread(image_own, "z", count)

    head = lax.optimization_barrier(panel[0] * on_col)
    head = head + lax.ppermute(head, "k", [(1, 0)])
    head = head + lax.ppermute(head, "x", [(0, 2)])
    came = lax.ppermute(head, "x", [(0, 1), (2, 3)])
    head = lax.optimization_barrier(head + came)

    refl_row = product(panel_row, inverse, ((1,), (1,))) + on_row
    image_row = product(mixed_row, inverse, ((1,), (1,))) + next_row
    refl = product(panel, inverse, ((2,), (1,))) + identity[None] * at_col[:, None, None]

    middle_part = packed(product(refl, image, ((0, 1), (0, 1)), FAST))
    came = spread(middle_part, COL, side)

    coupling = factor_call(
        inverse_kernel, 1, identity + product(inverse, head, ((1,), (1,)))
    )
    turned_row = product(refl_row, coupling, ((1,), (1,)))
    half_row = product(image_row, coupling, ((1,), (0,)))
    partial = lax.optimization_barrier(near.transpose(1, 0, 2) - product(turned_row, image, ((1,), (2,)), FAST))

    upper = jnp.sum(came[:, :half], axis=0)
    corner = came[:, half:]
    corner = jnp.concatenate([corner[:, :, :half], corner[:, :, half:]], axis=1)
    corner = jnp.sum(corner, axis=0)
    far = turned_row[:, half:]
    sandwich_row = product(turned_row[:, :half], upper, ((1,), (0,)))
    sandwich_row += jnp.concatenate(
        [
            product(far, upper[:, half:], ((1,), (1,))),
            product(far, corner, ((1,), (0,))),
        ],
        axis=1,
    )
    sandwich_row = product(sandwich_row, coupling, ((1,), (0,)))
    result = partial - product(half_row - sandwich_row, refl, ((1,), (2,)), FAST)
    return result[None]


def solution(mesh):
    grid = Mesh(mesh.devices.reshape(8, 8, 4, 2), ("z", "y", "x", "k"))
    spec = P(None, ("z", "y"), None, COL)

    return jax.shard_map(
        per_device, mesh=grid, in_specs=(spec,), out_specs=spec, check_vma=False
    )
```

```python
import jax
import jax.numpy as jnp
from jax import lax
from jax.experimental import pallas as pl
from jax.experimental.pallas import tpu as pltpu
from jax.sharding import Mesh, PartitionSpec as P

COL = ("x", "k")
PLANE = ("y", "x", "k")
FAST = lax.Precision.HIGH
BLOCK = 8
GROUP = 32


def product(left, right, contract, precision=lax.Precision.HIGHEST):
    return lax.dot_general(
        left,
        right,
        (contract, ((), ())),
        precision=precision,
        preferred_element_type=jnp.float32,
    )


def spread(block, axis, count):
    whole = jnp.broadcast_to(block[None], (count,) + block.shape)
    return lax.all_to_all(whole, axis, 0, 0, tiled=True)


def packed(square):
    half = square.shape[0] // 2
    corner = square[half:, half:]
    corner = jnp.concatenate([corner[: half // 2], corner[half // 2 :]], axis=1)
    return jnp.concatenate([square[:half], corner], axis=0)


def unit(width):
    rows = lax.broadcasted_iota(jnp.int32, (width, width), 0)
    lanes = lax.broadcasted_iota(jnp.int32, (width, width), 1)
    return (rows == lanes).astype(jnp.float32)


def first_kernel(matrix_ref, out_ref, tile, sem, sems):
    take = pltpu.make_async_copy(matrix_ref.at[0, :, 0, :], tile, sem)
    take.start()
    take.wait()
    spots = lax.axis_index("z") + lax.axis_index("y") + lax.axis_index("x")
    corner = spots + lax.axis_index("k") == 0
    tile[...] = jnp.where(corner, 0.0, tile[...])
    copies = [
        pltpu.make_async_copy(tile, out_ref.at[i], sems.at[i])
        for i in range(out_ref.shape[0])
    ]
    for copy in copies:
        copy.start()
    for copy in copies:
        copy.wait()


def first_call(matrix, count):
    width = matrix.shape[-1]
    return pl.pallas_call(
        first_kernel,
        out_shape=jax.ShapeDtypeStruct((count, width, width), jnp.float32),
        in_specs=[pl.BlockSpec(memory_space=pltpu.HBM)],
        out_specs=pl.BlockSpec(memory_space=pl.ANY),
        scratch_shapes=[
            pltpu.VMEM((width, width), jnp.float32),
            pltpu.SemaphoreType.DMA,
            pltpu.SemaphoreType.DMA((count,)),
        ],
        compiler_params=pltpu.CompilerParams(vmem_limit_bytes=2 << 20),
        name="first_tile",
    )(pltpu.with_memory_space_constraint(matrix, pltpu.HBM))


def shared_kernel(part_ref, gram_ref, out_ref):
    width = part_ref.shape[1]
    half, quarter = width // 2, width // 4
    gram = gram_ref[...]
    out_ref[:width, :] = part_ref[...]
    out_ref[width : width + half, :] = gram[:half]
    corner = [gram[half : half + quarter, half:], gram[half + quarter :, half:]]
    low = width + half
    out_ref[low:, :] = jnp.concatenate(corner, axis=1)


def shared_call(part, gram):
    width = part.shape[1]
    tall = width + width // 2 + width // 4
    return pl.pallas_call(
        shared_kernel,
        out_shape=jax.ShapeDtypeStruct((tall, width), jnp.float32),
        compiler_params=pltpu.CompilerParams(vmem_limit_bytes=2 << 20),
        name="shared",
    )(part, gram)


def columns_of(rows, low, width):
    return [
        jnp.broadcast_to(rows[:, low + b : low + b + 1], (BLOCK, width))
        for b in range(BLOCK)
    ]


def row_of(rows, j):
    return jnp.broadcast_to(rows[j : j + 1, :], rows.shape)


def cholesky_kernel(upper_ref, corner_ref, out_ref):
    width = out_ref.shape[0]
    half = width // 2
    upper, corner = upper_ref[...], corner_ref[...]
    lower = jnp.concatenate(
        [jnp.zeros((half, half), jnp.float32)]
        + [jnp.concatenate([corner[:, :half], corner[:, half:]], axis=0)],
        axis=1,
    )
    gram = jnp.concatenate([upper, lower], axis=0)
    lanes = lax.broadcasted_iota(jnp.int32, (1, width), 1)
    place = lax.broadcasted_iota(jnp.int32, (BLOCK, 1), 0)
    turned = gram.T
    rows = []
    for low in range(0, width, BLOCK):
        own = gram[low : low + BLOCK, :]
        if low >= half:
            own = jnp.where(lanes < half, turned[low : low + BLOCK, :], own)
        rows.append(own)
    count = width // BLOCK
    for i in range(count):
        low = BLOCK * i
        live = range(i, count)
        cols = {v: columns_of(rows[v], low, width) for v in live}
        inside = (lanes >= low) & (lanes < low + BLOCK)
        for v in live:
            fill = (lanes == low + place).astype(jnp.float32) if v == i else 0.0
            rows[v] = jnp.where(inside, fill, rows[v])
        for j in range(BLOCK):
            scale = lax.rsqrt(row_of(cols[i][j], j))
            pivots = [
                row_of(cols[i][b], j) * scale if b > j else None for b in range(BLOCK)
            ]
            pivot = row_of(rows[i], j) * scale
            for v in live:
                factor = cols[v][j] * scale
                if v == i:
                    factor = jnp.where(place > j, factor, 0.0)
                for b in range(j + 1, BLOCK):
                    cols[v][b] = cols[v][b] - factor * pivots[b]
                after = rows[v] - factor * pivot
                rows[v] = jnp.where(place == j, pivot, after) if v == i else after
        out_ref[low : low + BLOCK, :] = jnp.where(lanes < low + BLOCK, rows[i], 0.0)


def inverse_kernel(matrix_ref, out_ref, work):
    width = out_ref.shape[0]
    work[...] = matrix_ref[...]
    lanes = lax.broadcasted_iota(jnp.int32, (1, width), 1)
    place = lax.broadcasted_iota(jnp.int32, (BLOCK, 1), 0)
    count = GROUP // BLOCK
    for top in range(0, width, GROUP):
        rows = [work[top + BLOCK * v : top + BLOCK * (v + 1), :] for v in range(count)]
        for i in range(count):
            low = top + BLOCK * i
            cols = [columns_of(rows[v], low, width) for v in range(count)]
            inside = (lanes >= low) & (lanes < low + BLOCK)
            for v in range(count):
                fill = (lanes == low + place).astype(jnp.float32) if v == i else 0.0
                rows[v] = jnp.where(inside, fill, rows[v])
            for j in range(BLOCK):
                scale = 1.0 / row_of(cols[i][j], j)
                pivots = [
                    row_of(cols[i][b], j) * scale if b > j else None
                    for b in range(BLOCK)
                ]
                pivot = row_of(rows[i], j) * scale
                for v in range(count):
                    factor = cols[v][j]
                    for b in range(j + 1, BLOCK):
                        after = cols[v][b] - factor * pivots[b]
                        if v == i:
                            after = jnp.where(place == j, pivots[b], after)
                        cols[v][b] = after
                    after = rows[v] - factor * pivot
                    rows[v] = jnp.where(place == j, pivot, after) if v == i else after
        group = jnp.concatenate(rows, axis=0)
        inside = (lanes >= top) & (lanes < top + GROUP)
        for start, stop in ((0, top), (top + GROUP, width)):
            if stop > start:
                old = work[start:stop, :]
                work[start:stop, :] = jnp.where(inside, 0.0, old) - product(
                    old[:, top : top + GROUP], group, ((1,), (0,))
                )
        work[top : top + GROUP, :] = group
    out_ref[...] = work[...]


def transposition(side):
    def ring(a, b, size):
        return min((a - b) % size, (b - a) % size)

    pairs = []
    for c in range(side):
        targets = sorted(range(side), key=lambda y: -ring(y, c, side))
        sources = sorted(range(side), key=lambda d: ring(d // 2, c // 2, side // 2))
        pairs += [(c * side + d, y * side + c) for d, y in zip(sources, targets)]
    return pairs


def factor_call(kernel, scratch, *operands):
    width = operands[0].shape[1]
    return pl.pallas_call(
        kernel,
        out_shape=jax.ShapeDtypeStruct((width, width), jnp.float32),
        scratch_shapes=[pltpu.VMEM((width, width), jnp.float32)] * scratch,
        cost_estimate=pl.CostEstimate(
            flops=0, bytes_accessed=30_000_000, transcendentals=0
        ),
        compiler_params=pltpu.CompilerParams(vmem_limit_bytes=4 << 20),
    )(*operands)


def per_device(matrix):
    _, width, count, _ = matrix.shape
    side = lax.axis_size("y")
    row = lax.axis_index("z") * side + lax.axis_index("y")
    col = lax.axis_index(COL)
    swap = transposition(side)
    half = width // 2
    local = matrix[0]

    on_row = lax.optimization_barrier(unit(width) * (row == 1))
    on_col = lax.optimization_barrier((col == 1).astype(jnp.float32))
    at_col = (jnp.arange(count) == 0).astype(jnp.float32) * on_col
    at_col = lax.optimization_barrier(at_col)
    identity = unit(width)

    first = lax.all_to_all(first_call(matrix, side), COL, 0, 0, tiled=True)
    panel_row = first[0]
    next_row = first[1]
    panel_own = lax.ppermute(panel_row, PLANE, swap)
    near = lax.optimization_barrier(jnp.transpose(local, (1, 0, 2)))
    panel = spread(panel_own, "z", count)
    next_own = lax.ppermute(next_row, PLANE, swap)

    part = product(near, panel, ((0, 2), (0, 1)))
    gram_part = product(panel, panel, ((0, 1), (0, 1)))
    shared = shared_call(part, gram_part)
    total = jnp.sum(spread(shared, COL, side), axis=0)
    mixed_row = total[:width]
    mixed_own = lax.ppermute(mixed_row, PLANE, swap)
    inverse = factor_call(
        cholesky_kernel, 0, total[width : width + half], total[width + half :]
    )

    image_own = product(mixed_own, inverse, ((1,), (1,))) + next_own
    image = spread(image_own, "z", count)

    head = lax.optimization_barrier(panel[0] * on_col)
    head = head + lax.ppermute(head, "k", [(1, 0)])
    head = head + lax.ppermute(head, "x", [(0, 2)])
    came = lax.ppermute(head, "x", [(0, 1), (2, 3)])
    head = lax.optimization_barrier(head + came)

    refl_row = product(panel_row, inverse, ((1,), (1,))) + on_row
    image_row = product(mixed_row, inverse, ((1,), (1,))) + next_row
    refl = product(panel, inverse, ((2,), (1,))) + identity[None] * at_col[:, None, None]

    middle_part = packed(product(refl, image, ((0, 1), (0, 1)), FAST))
    came = spread(middle_part, COL, side)

    coupling = factor_call(
        inverse_kernel, 1, identity + product(inverse, head, ((1,), (1,)))
    )
    turned_row = product(refl_row, coupling, ((1,), (1,)))
    half_row = product(image_row, coupling, ((1,), (0,)))
    partial = lax.optimization_barrier(near.transpose(1, 0, 2) - product(turned_row, image, ((1,), (2,)), FAST))

    upper = jnp.sum(came[:, :half], axis=0)
    corner = came[:, half:]
    corner = jnp.concatenate([corner[:, :, :half], corner[:, :, half:]], axis=1)
    corner = jnp.sum(corner, axis=0)
    far = turned_row[:, half:]
    sandwich_row = product(turned_row[:, :half], upper, ((1,), (0,)))
    sandwich_row += jnp.concatenate(
        [
            product(far, upper[:, half:], ((1,), (1,))),
            product(far, corner, ((1,), (0,))),
        ],
        axis=1,
    )
    sandwich_row = product(sandwich_row, coupling, ((1,), (0,)))
    result = partial - product(half_row - sandwich_row, refl, ((1,), (2,)), FAST)
    return result[None]


def solution(mesh):
    grid = Mesh(mesh.devices.reshape(8, 8, 4, 2), ("z", "y", "x", "k"))
    spec = P(None, ("z", "y"), None, COL)

    return jax.shard_map(
        per_device, mesh=grid, in_specs=(spec,), out_specs=spec, check_vma=False
    )
```

```python
import jax
import jax.numpy as jnp
from jax import lax
from jax.experimental import pallas as pl
from jax.experimental.pallas import tpu as pltpu
from jax.sharding import Mesh, PartitionSpec as P

COL = ("x", "k")
PLANE = ("y", "x", "k")
FAST = lax.Precision.HIGH
BLOCK = 8
GROUP = 32


def product(left, right, contract, precision=lax.Precision.HIGHEST):
    return lax.dot_general(
        left,
        right,
        (contract, ((), ())),
        precision=precision,
        preferred_element_type=jnp.float32,
    )


def spread(block, axis, count):
    whole = jnp.broadcast_to(block[None], (count,) + block.shape)
    return lax.all_to_all(whole, axis, 0, 0, tiled=True)


def packed(square):
    half = square.shape[0] // 2
    corner = square[half:, half:]
    corner = jnp.concatenate([corner[: half // 2], corner[half // 2 :]], axis=1)
    return jnp.concatenate([square[:half], corner], axis=0)


def unit(width):
    rows = lax.broadcasted_iota(jnp.int32, (width, width), 0)
    lanes = lax.broadcasted_iota(jnp.int32, (width, width), 1)
    return (rows == lanes).astype(jnp.float32)


def first_kernel(matrix_ref, out_ref, tile, sem, sems):
    take = pltpu.make_async_copy(matrix_ref.at[0, :, 0, :], tile, sem)
    take.start()
    take.wait()
    spots = lax.axis_index("z") + lax.axis_index("y") + lax.axis_index("x")
    corner = spots + lax.axis_index("k") == 0
    tile[...] = jnp.where(corner, 0.0, tile[...])
    copies = [
        pltpu.make_async_copy(tile, out_ref.at[i], sems.at[i])
        for i in range(out_ref.shape[0])
    ]
    for copy in copies:
        copy.start()
    for copy in copies:
        copy.wait()


def first_call(matrix, count):
    width = matrix.shape[-1]
    return pl.pallas_call(
        first_kernel,
        out_shape=jax.ShapeDtypeStruct((count, width, width), jnp.float32),
        in_specs=[pl.BlockSpec(memory_space=pltpu.HBM)],
        out_specs=pl.BlockSpec(memory_space=pl.ANY),
        scratch_shapes=[
            pltpu.VMEM((width, width), jnp.float32),
            pltpu.SemaphoreType.DMA,
            pltpu.SemaphoreType.DMA((count,)),
        ],
        compiler_params=pltpu.CompilerParams(vmem_limit_bytes=2 << 20),
        name="first_tile",
    )(pltpu.with_memory_space_constraint(matrix, pltpu.HBM))


def shared_kernel(part_ref, gram_ref, out_ref):
    width = part_ref.shape[1]
    half, quarter = width // 2, width // 4
    gram = gram_ref[...]
    out_ref[:width, :] = part_ref[...]
    out_ref[width : width + half, :] = gram[:half]
    corner = [gram[half : half + quarter, half:], gram[half + quarter :, half:]]
    low = width + half
    out_ref[low:, :] = jnp.concatenate(corner, axis=1)


def shared_call(part, gram):
    width = part.shape[1]
    tall = width + width // 2 + width // 4
    return pl.pallas_call(
        shared_kernel,
        out_shape=jax.ShapeDtypeStruct((tall, width), jnp.float32),
        compiler_params=pltpu.CompilerParams(vmem_limit_bytes=2 << 20),
        name="shared",
    )(part, gram)


def columns_of(rows, low, width):
    return [
        jnp.broadcast_to(rows[:, low + b : low + b + 1], (BLOCK, width))
        for b in range(BLOCK)
    ]


def row_of(rows, j):
    return jnp.broadcast_to(rows[j : j + 1, :], rows.shape)


def cholesky_kernel(upper_ref, corner_ref, out_ref):
    width = out_ref.shape[0]
    half = width // 2
    upper, corner = upper_ref[...], corner_ref[...]
    lower = jnp.concatenate(
        [jnp.zeros((half, half), jnp.float32)]
        + [jnp.concatenate([corner[:, :half], corner[:, half:]], axis=0)],
        axis=1,
    )
    gram = jnp.concatenate([upper, lower], axis=0)
    lanes = lax.broadcasted_iota(jnp.int32, (1, width), 1)
    place = lax.broadcasted_iota(jnp.int32, (BLOCK, 1), 0)
    turned = gram.T
    rows = []
    for low in range(0, width, BLOCK):
        own = gram[low : low + BLOCK, :]
        if low >= half:
            own = jnp.where(lanes < half, turned[low : low + BLOCK, :], own)
        rows.append(own)
    count = width // BLOCK
    for i in range(count):
        low = BLOCK * i
        live = range(i, count)
        cols = {v: columns_of(rows[v], low, width) for v in live}
        inside = (lanes >= low) & (lanes < low + BLOCK)
        for v in live:
            fill = (lanes == low + place).astype(jnp.float32) if v == i else 0.0
            rows[v] = jnp.where(inside, fill, rows[v])
        for j in range(BLOCK):
            scale = lax.rsqrt(row_of(cols[i][j], j))
            pivots = [
                row_of(cols[i][b], j) * scale if b > j else None for b in range(BLOCK)
            ]
            pivot = row_of(rows[i], j) * scale
            for v in live:
                factor = cols[v][j] * scale
                if v == i:
                    factor = jnp.where(place > j, factor, 0.0)
                for b in range(j + 1, BLOCK):
                    cols[v][b] = cols[v][b] - factor * pivots[b]
                after = rows[v] - factor * pivot
                rows[v] = jnp.where(place == j, pivot, after) if v == i else after
        out_ref[low : low + BLOCK, :] = jnp.where(lanes < low + BLOCK, rows[i], 0.0)


def inverse_kernel(matrix_ref, out_ref, work):
    width = out_ref.shape[0]
    work[...] = matrix_ref[...]
    lanes = lax.broadcasted_iota(jnp.int32, (1, width), 1)
    place = lax.broadcasted_iota(jnp.int32, (BLOCK, 1), 0)
    count = GROUP // BLOCK
    for top in range(0, width, GROUP):
        rows = [work[top + BLOCK * v : top + BLOCK * (v + 1), :] for v in range(count)]
        for i in range(count):
            low = top + BLOCK * i
            cols = [columns_of(rows[v], low, width) for v in range(count)]
            inside = (lanes >= low) & (lanes < low + BLOCK)
            for v in range(count):
                fill = (lanes == low + place).astype(jnp.float32) if v == i else 0.0
                rows[v] = jnp.where(inside, fill, rows[v])
            for j in range(BLOCK):
                scale = 1.0 / row_of(cols[i][j], j)
                pivots = [
                    row_of(cols[i][b], j) * scale if b > j else None
                    for b in range(BLOCK)
                ]
                pivot = row_of(rows[i], j) * scale
                for v in range(count):
                    factor = cols[v][j]
                    for b in range(j + 1, BLOCK):
                        after = cols[v][b] - factor * pivots[b]
                        if v == i:
                            after = jnp.where(place == j, pivots[b], after)
                        cols[v][b] = after
                    after = rows[v] - factor * pivot
                    rows[v] = jnp.where(place == j, pivot, after) if v == i else after
        group = jnp.concatenate(rows, axis=0)
        inside = (lanes >= top) & (lanes < top + GROUP)
        for start, stop in ((0, top), (top + GROUP, width)):
            if stop > start:
                old = work[start:stop, :]
                work[start:stop, :] = jnp.where(inside, 0.0, old) - product(
                    old[:, top : top + GROUP], group, ((1,), (0,))
                )
        work[top : top + GROUP, :] = group
    out_ref[...] = work[...]


def transposition(side):
    def ring(a, b, size):
        return min((a - b) % size, (b - a) % size)

    pairs = []
    for c in range(side):
        targets = sorted(range(side), key=lambda y: -ring(y, c, side))
        sources = sorted(range(side), key=lambda d: ring(d // 2, c // 2, side // 2))
        pairs += [(c * side + d, y * side + c) for d, y in zip(sources, targets)]
    return pairs


def factor_call(kernel, scratch, *operands):
    width = operands[0].shape[1]
    return pl.pallas_call(
        kernel,
        out_shape=jax.ShapeDtypeStruct((width, width), jnp.float32),
        scratch_shapes=[pltpu.VMEM((width, width), jnp.float32)] * scratch,
        cost_estimate=pl.CostEstimate(
            flops=0, bytes_accessed=30_000_000, transcendentals=0
        ),
        compiler_params=pltpu.CompilerParams(vmem_limit_bytes=4 << 20),
    )(*operands)


def per_device(matrix):
    _, width, count, _ = matrix.shape
    side = lax.axis_size("y")
    row = lax.axis_index("z") * side + lax.axis_index("y")
    col = lax.axis_index(COL)
    swap = transposition(side)
    half = width // 2
    local = matrix[0]

    on_row = lax.optimization_barrier(unit(width) * (row == 1))
    on_col = lax.optimization_barrier((col == 1).astype(jnp.float32))
    at_col = (jnp.arange(count) == 0).astype(jnp.float32) * on_col
    at_col = lax.optimization_barrier(at_col)
    identity = unit(width)

    first = lax.all_to_all(first_call(matrix, side), COL, 0, 0, tiled=True)
    panel_row = first[0]
    next_row = first[1]
    panel_own = lax.ppermute(panel_row, PLANE, swap)
    near = lax.optimization_barrier(jnp.transpose(local, (1, 0, 2)))
    panel = spread(panel_own, "z", count)
    next_own = lax.ppermute(next_row, PLANE, swap)

    part = product(near, panel, ((0, 2), (0, 1)))
    gram_part = product(panel, panel, ((0, 1), (0, 1)))
    shared = shared_call(part, gram_part)
    total = jnp.sum(spread(shared, COL, side), axis=0)
    mixed_row = total[:width]
    mixed_own = lax.ppermute(mixed_row, PLANE, swap)
    inverse = factor_call(
        cholesky_kernel, 0, total[width : width + half], total[width + half :]
    )

    image_own = product(mixed_own, inverse, ((1,), (1,))) + next_own
    image = spread(image_own, "z", count)

    head = lax.optimization_barrier(panel[0] * on_col)
    head = head + lax.ppermute(head, "k", [(1, 0)])
    head = head + lax.ppermute(head, "x", [(0, 2)])
    came = lax.ppermute(head, "x", [(0, 1), (2, 3)])
    head = lax.optimization_barrier(head + came)

    refl_row = product(panel_row, inverse, ((1,), (1,))) + on_row
    image_row = product(mixed_row, inverse, ((1,), (1,))) + next_row
    refl = product(panel, inverse, ((2,), (1,))) + identity[None] * at_col[:, None, None]

    middle_part = packed(product(refl, image, ((0, 1), (0, 1)), FAST))
    came = spread(middle_part, COL, side)

    coupling = factor_call(
        inverse_kernel, 1, identity + product(inverse, head, ((1,), (1,)))
    )
    turned_row = product(refl_row, coupling, ((1,), (1,)))
    half_row = product(image_row, coupling, ((1,), (0,)))
    partial = lax.optimization_barrier(near.transpose(1, 0, 2) - product(turned_row, image, ((1,), (2,)), FAST))

    upper = jnp.sum(came[:, :half], axis=0)
    corner = came[:, half:]
    corner = jnp.concatenate([corner[:, :, :half], corner[:, :, half:]], axis=1)
    corner = jnp.sum(corner, axis=0)
    far = turned_row[:, half:]
    sandwich_row = product(turned_row[:, :half], upper, ((1,), (0,)), FAST)
    sandwich_row += jnp.concatenate(
        [
            product(far, upper[:, half:], ((1,), (1,)), FAST),
            product(far, corner, ((1,), (0,)), FAST),
        ],
        axis=1,
    )
    sandwich_row = product(sandwich_row, coupling, ((1,), (0,)), FAST)
    result = partial - product(half_row - sandwich_row, refl, ((1,), (2,)), FAST)
    return result[None]


def solution(mesh):
    grid = Mesh(mesh.devices.reshape(8, 8, 4, 2), ("z", "y", "x", "k"))
    spec = P(None, ("z", "y"), None, COL)

    return jax.shard_map(
        per_device, mesh=grid, in_specs=(spec,), out_specs=spec, check_vma=False
    )
```
